256 devices in a mesh: tm: 32 (over x, y, core), rows: 8 (over z).
Axes of the slice: x: 4, y: 4, z: 8, core: 2. Of those that a mesh axis runs over, the one named last changes fastest.
Arguments:
- latents: bfloat16 [64, 32, 64, 512], P('tm', 'rows'), may hold values from -128 to 128
- conv_weight: bfloat16 [27, 512, 512], P(None, 'tm'), may hold values from -0.0546875 to 0.0546875
- query_weight: bfloat16 [512, 512], replicated, may hold values from -1 to 4
- key_weight: bfloat16 [512, 512], replicated, may hold values from -1 to 4
- value_weight: bfloat16 [512, 512], replicated, may hold values from -0.25 to 0.25
- out_weight: bfloat16 [512, 512], replicated, may hold values from -1.5 to 1.5
Outputs:
- output: bfloat16 [64, 32, 64, 512], P('tm', 'rows')
The draws below stay inside these ranges and needn't reach their ends.
All inputs are finite; a program needn't handle non-finite values.
Results may differ from the reference program's by a relative error of at most 0.028.
Values may be sent and summed in bfloat16 or wider, within the bound.
A program may use at most 128 MiB of HBM per device.

```python
import math
import jax
import jax.numpy as jnp
from jax import lax

C = 512
G = 32
W = 64
FRAMES = 64
H = 32


def draw_latents(key, part):
    first = jax.random.fold_in(key, 21)
    second = jax.random.fold_in(key, 22)
    third = jax.random.fold_in(key, 23)
    position = jnp.arange(H, dtype=jnp.float32) / max(H - 1, 1)
    roughness = jnp.exp(jax.random.uniform(first, (FRAMES, H, 1, 1), jnp.float32) * math.log(2.0))
    channel_scale = jnp.exp(jax.random.uniform(third, (1, 1, 1, C), jnp.float32) * math.log(3.0))
    rising = (3.0 ** position)[None, :, None, None]
    entries = jax.random.truncated_normal(second, -4.0, 4.0, (FRAMES, H, W, C), jnp.float32)
    return ((entries + 0.5) * rising * roughness * channel_scale).astype(jnp.bfloat16)


def drawn_weight(key, constant):
    random_part = jax.random.truncated_normal(jax.random.fold_in(key, constant), -6.0, 6.0, (C, C), jnp.float32) / math.sqrt(C)
    return random_part.astype(jnp.bfloat16)


def draw_query_weight(key, part):
    return drawn_weight(key, 31)


def draw_key_weight(key, part):
    return drawn_weight(key, 32)


def steps_of(stream_key, dims, shards, least, largest):
    def one(dim, blocks):
        heights = jax.random.uniform(jax.random.fold_in(jax.random.fold_in(stream_key, 6), dim), (blocks,), jnp.float32, least / len(shards), largest / len(shards))
        return jnp.repeat(jnp.exp(heights), dims[dim] // blocks).reshape((-1,) + (1,) * (len(dims) - dim - 1))

    loudness = one(*shards[0])
    for cut in shards[1:]:
        loudness = loudness * one(*cut)
    return loudness


def noise(key, shape, scale, most, pieces=(), held_as=jnp.bfloat16):
    array = scale * jax.random.normal(key, shape, jnp.float32)
    if pieces:
        array = array * steps_of(key, shape, pieces, -0.22, 0.18)
    return jnp.clip(array, -most, most).astype(held_as)


def setup_inputs(seed: int = 0) -> dict:
    key_list = jax.random.split(jax.random.key(seed), 7)
    return {
        "latents": draw_latents(jax.random.fold_in(key_list[6], 71), 0),
        "conv_weight": noise(key_list[1], (27, C, C), (27 * C) ** -0.5, 0.0546875, ((1, 32),)),
        "query_weight": draw_query_weight(jax.random.fold_in(key_list[6], 71), 0),
        "key_weight": draw_key_weight(jax.random.fold_in(key_list[6], 71), 0),
        "value_weight": noise(key_list[4], (C, C), C ** -0.5, 0.25),
        "out_weight": noise(key_list[5], (C, C), (C // 36) ** -0.5, 1.5),
    }


epsilon = 1e-06

def frame_block(window, conv_weight, query_weight, key_weight, value_weight, out_weight):
    totals = jnp.zeros((H * W, C), jnp.float32)
    for tap_index in range(27):
        frame_lag = tap_index // 9
        row_lag = tap_index // 3 % 3
        col_lag = tap_index % 3
        patches = window[frame_lag, row_lag:row_lag + H, col_lag:col_lag + W, :].reshape(H * W, C)
        totals = totals + jnp.dot(patches, conv_weight[tap_index], preferred_element_type=jnp.float32)
    convolved = totals.astype(jnp.bfloat16)
    grouped = convolved.astype(jnp.float32).reshape(H * W, G, C // G)
    average = lax.optimization_barrier(jnp.mean(grouped, axis=(0, 2)))
    centered = grouped - average[None, :, None]
    variance = lax.optimization_barrier(jnp.mean(centered * centered, axis=(0, 2)))
    normed = (centered * lax.rsqrt(variance + epsilon)[None, :, None]).reshape(H * W, C).astype(jnp.bfloat16)
    queries = jnp.dot(normed, query_weight, preferred_element_type=jnp.float32).astype(jnp.bfloat16)
    keys = jnp.dot(normed, key_weight, preferred_element_type=jnp.float32).astype(jnp.bfloat16)
    values = jnp.dot(normed, value_weight, preferred_element_type=jnp.float32).astype(jnp.bfloat16)
    scores = jnp.dot(queries, keys.T, preferred_element_type=jnp.float32) * C ** (-0.5)
    row_max = lax.optimization_barrier(jnp.max(scores, axis=1, keepdims=True))
    exp_weights = jnp.exp(scores - row_max).astype(jnp.bfloat16)
    denominator = lax.optimization_barrier(jnp.sum(exp_weights.astype(jnp.float32), axis=1, keepdims=True))
    numerator = jnp.dot(exp_weights, values, preferred_element_type=jnp.float32)
    attended = (numerator / denominator).astype(jnp.bfloat16)
    summed = convolved.astype(jnp.float32) + jnp.dot(attended, out_weight, preferred_element_type=jnp.float32)
    return summed.astype(jnp.bfloat16).reshape(H, W, C)

def reference(latents, conv_weight, query_weight, key_weight, value_weight, out_weight):
    padded = jnp.pad(latents, ((2, 0), (1, 1), (1, 1), (0, 0)))

    def one_frame(frame_index):
        window = lax.dynamic_slice_in_dim(padded, frame_index, 3, 0)
        return frame_block(window, conv_weight, query_weight, key_weight, value_weight, out_weight)
    return lax.map(one_frame, jnp.arange(FRAMES, dtype=jnp.int32))
```

```python
import functools

import jax
import jax.numpy as jnp
from jax import lax
from jax.experimental import pallas as pl
from jax.experimental.pallas import tpu as pltpu
from jax.sharding import PartitionSpec as P

MESH = pl.DeviceIdType.MESH
F32 = jnp.float32
BF16 = jnp.bfloat16

GROUPS = 32
EPSILON = 1e-06
LOG2E = 1.4426950408889634
NX, NY, NC, NZ = 4, 4, 2, 8
TAPS = 27
CHUNKS = 4

A, A1, A2 = (0, 14), (0, 7), (7, 7)
B, B1, B2 = (14, 13), (14, 7), (21, 6)


def kernel(
    lat, cw, wq, wk, wv, wo, out,
    raw, win, w, kv, acc, st, wts, qq, qb, mx, den, num,
    w_send, w_recv, d_send, d_recv, z_send, z_recv, h_send, h_recv, s_send, s_recv, loc,
):
    tm = lax.axis_index("tm")
    z = lax.axis_index("rows")
    x, y, core = tm // (NY * NC), tm // NC % NY, tm % NC
    mate = tm + 1 - 2 * core
    ntm = NX * NY * NC

    def at(px, py):
        return (px * NY + py) * NC + core

    def xs(d):
        return (x + d + NX) % NX

    def ys(d):
        return (y + d + NY) % NY

    def zs(d):
        return (z + d + NZ) % NZ

    def copy(src, dst, ss, rs, to_tm, to_z):
        return pltpu.make_async_remote_copy(
            src_ref=src, dst_ref=dst, send_sem=ss, recv_sem=rs,
            device_id={"tm": to_tm, "rows": to_z}, device_id_type=MESH,
        )

    sent = []

    def send(src, dst, ss, rs, to_tm, to_z):
        c = copy(src, dst, ss, rs, to_tm, to_z)
        c.start()
        sent.append((src, ss))

    def arrived(ref, rs):
        copy(ref, ref, rs, rs, mate, z).wait_recv()

    barrier = pltpu.get_barrier_semaphore()
    peers = [(at(xs(1), y), z), (at(xs(-1), y), z), (at(x, ys(1)), z), (at(x, ys(-1)), z)]
    peers += [(mate, z), ((tm + 1) % ntm, z), ((tm + ntm - 1) % ntm, z)]
    peers += [(tm, zs(d)) for d in range(1, NZ)]
    for ptm, pz in peers:
        pl.semaphore_signal(barrier, inc=1, device_id={"tm": ptm, "rows": pz}, device_id_type=MESH)
    pl.semaphore_wait(barrier, len(peers))

    chans = lat.shape[3]
    cols = chans // CHUNKS

    def own(j, part):
        return cw.at[part[0] : part[0] + part[1], :, j * cols : (j + 1) * cols]

    def piece(j, px, py, part):
        return w.at[j, px, py, core, part[0] : part[0] + part[1]]

    def line_x(j, py, part):
        return w.at[j, :, py, core, part[0] : part[0] + part[1]]

    def line_y(j, px, part):
        return w.at[j, px, :, core, part[0] : part[0] + part[1]]

    def sems(j, r):
        return [(w_send.at[j, r, i], w_recv.at[j, r, i]) for i in range(4)]

    def start_1a(j):
        s = sems(j, 0)
        send(own(j, A), piece(j, x, y, A), *s[0], at(xs(1), y), z)
        send(own(j, B), piece(j, x, y, B), *s[2], at(x, ys(1)), z)
        send(own(j, A), piece(j, x, y, A), *s[1], at(xs(-1), y), z)
        send(own(j, B), piece(j, x, y, B), *s[3], at(x, ys(-1)), z)

    def start_1b(j):
        r = w_recv
        arrived(piece(j, xs(-1), y, A), r.at[j, 0, 0])
        s = sems(j, 1)
        src = piece(j, xs(-1), y, A1)
        send(src, src, *s[0], at(xs(1), y), z)
        arrived(piece(j, x, ys(-1), B), r.at[j, 0, 2])
        src = piece(j, x, ys(-1), B1)
        send(src, src, *s[2], at(x, ys(1)), z)
        arrived(piece(j, xs(1), y, A), r.at[j, 0, 1])
        src = piece(j, xs(1), y, A2)
        send(src, src, *s[1], at(xs(-1), y), z)
        arrived(piece(j, x, ys(1), B), r.at[j, 0, 3])
        src = piece(j, x, ys(1), B2)
        send(src, src, *s[3], at(x, ys(-1)), z)

    def to_mate(j, i, ref):
        send(ref, ref, d_send.at[j, i], d_recv.at[j, i], mate, z)

    def start_2a(j):
        r = w_recv
        arrived(piece(j, xs(2), y, A1), r.at[j, 1, 0])
        arrived(piece(j, xs(2), y, A2), r.at[j, 1, 1])
        arrived(piece(j, x, ys(2), B1), r.at[j, 1, 2])
        arrived(piece(j, x, ys(2), B2), r.at[j, 1, 3])
        pltpu.make_async_copy(
            cw.at[:, :, j * cols : (j + 1) * cols], w.at[j, x, y, core], loc.at[j]
        ).wait()
        s = sems(j, 2)
        la, lb = line_x(j, y, A), line_y(j, x, B)
        send(la, la, *s[0], at(x, ys(1)), z)
        send(lb, lb, *s[2], at(xs(1), y), z)
        send(la, la, *s[1], at(x, ys(-1)), z)
        send(lb, lb, *s[3], at(xs(-1), y), z)
        to_mate(j, 0, la)
        to_mate(j, 1, lb)

    def start_2b(j):
        r = w_recv
        s = sems(j, 3)
        arrived(line_x(j, ys(-1), A), r.at[j, 2, 0])
        src = line_x(j, ys(-1), A1)
        send(src, src, *s[0], at(x, ys(1)), z)
        arrived(line_y(j, xs(-1), B), r.at[j, 2, 2])
        src = line_y(j, xs(-1), B1)
        send(src, src, *s[2], at(xs(1), y), z)
        arrived(line_x(j, ys(1), A), r.at[j, 2, 1])
        src = line_x(j, ys(1), A2)
        send(src, src, *s[1], at(x, ys(-1)), z)
        arrived(line_y(j, xs(1), B), r.at[j, 2, 3])
        src = line_y(j, xs(1), B2)
        send(src, src, *s[3], at(xs(-1), y), z)
        to_mate(j, 2, line_x(j, ys(-1), A))
        to_mate(j, 3, line_y(j, xs(-1), B))
        to_mate(j, 4, line_x(j, ys(1), A))
        to_mate(j, 5, line_y(j, xs(1), B))

    def finish_gather(j):
        r = w_recv
        arrived(line_x(j, ys(2), A1), r.at[j, 3, 0])
        arrived(line_x(j, ys(2), A2), r.at[j, 3, 1])
        to_mate(j, 6, line_x(j, ys(2), A))
        arrived(line_y(j, xs(2), B1), r.at[j, 3, 2])
        arrived(line_y(j, xs(2), B2), r.at[j, 3, 3])
        to_mate(j, 7, line_y(j, xs(2), B))
        other = 1 - core
        for i, (d, whole) in enumerate(
            ((0, True), (0, False), (-1, True), (-1, False), (1, True), (1, False), (2, True), (2, False))
        ):
            if whole:
                ref = w.at[j, :, ys(d), other, A[0] : A[0] + A[1]]
            else:
                ref = w.at[j, xs(d), :, other, B[0] : B[0] + B[1]]
            arrived(ref, d_recv.at[j, i])

    def z_send_pair(j, r, up, down):
        send(up, up, z_send.at[j, r, 0], z_recv.at[j, r, 0], tm, zs(1))
        send(down, down, z_send.at[j, r, 1], z_recv.at[j, r, 1], tm, zs(-1))

    def z_step(j, r):
        if r == 0:
            z_send_pair(j, 0, kv.at[j, z], kv.at[j, z])
            return
        if r < 4:
            from_low, from_high = kv.at[j, zs(-r)], kv.at[j, zs(r)]
        else:
            from_low, from_high = kv.at[j, zs(4), 0], kv.at[j, zs(4), 1]
        arrived(from_low, z_recv.at[j, r - 1, 0])
        arrived(from_high, z_recv.at[j, r - 1, 1])
        if r < 3:
            z_send_pair(j, r, from_low, from_high)
        elif r == 3:
            z_send_pair(j, 3, kv.at[j, zs(-3), 0], kv.at[j, zs(3), 1])

    start_1a(0)
    locals_ = [pltpu.make_async_copy(lat, raw.at[2:4, 1:5], loc.at[CHUNKS])]
    for j in range(CHUNKS):
        locals_.append(
            pltpu.make_async_copy(cw.at[:, :, j * cols : (j + 1) * cols], w.at[j, x, y, core], loc.at[j])
        )
    for i, m in enumerate((wq, wk, wv, wo)):
        locals_.append(pltpu.make_async_copy(m, wts.at[i], loc.at[CHUNKS + 1 + i]))
    nxt = (tm + 1) % ntm
    send(lat.at[:, 0], raw.at[0:2, 1], h_send.at[0], h_recv.at[0], nxt, z)
    send(lat.at[:, 3], raw.at[0:2, 4], h_send.at[1], h_recv.at[1], nxt, z)
    send(lat.at[:, 1:3], raw.at[0:2, 2:4], h_send.at[2], h_recv.at[2], nxt, z)
    send(lat.at[:, 0], raw.at[2:4, 5], h_send.at[3], h_recv.at[3], tm, zs(-1))
    send(lat.at[:, 3], raw.at[2:4, 0], h_send.at[4], h_recv.at[4], tm, zs(1))
    for c in locals_:
        c.start()

    start_1b(0)
    start_2a(0)
    start_1a(1)
    arrived(raw.at[0:2, 1], h_recv.at[0])
    send(raw.at[0:2, 1], raw.at[0:2, 5], h_send.at[5], h_recv.at[5], tm, zs(-1))
    arrived(raw.at[0:2, 4], h_recv.at[1])
    send(raw.at[0:2, 4], raw.at[0:2, 0], h_send.at[6], h_recv.at[6], tm, zs(1))
    start_1b(1)
    start_2b(0)
    start_2a(1)
    start_1a(2)
    arrived(raw.at[0:2, 2:4], h_recv.at[2])
    arrived(raw.at[2:4, 5], h_recv.at[3])
    arrived(raw.at[2:4, 0], h_recv.at[4])
    arrived(raw.at[0:2, 5], h_recv.at[5])
    arrived(raw.at[0:2, 0], h_recv.at[6])
    locals_[0].wait()

    col = lax.broadcasted_iota(jnp.int32, (lat.shape[2], chans), 0)

    def shift(i, carry):
        f, r = i // 6, i % 6
        outside = ((r == 0) & (z == 0)) | ((r == 5) & (z == NZ - 1)) | ((f < 2) & (tm == 0))
        keep = jnp.where(outside, 0.0, 1.0).astype(F32)
        v = raw[f, r].astype(F32) * keep
        win[1, f, r] = v.astype(BF16)
        last = lat.shape[2] - 1
        win[0, f, r] = jnp.where(col == 0, 0.0, pltpu.roll(v, 1, 0)).astype(BF16)
        win[2, f, r] = jnp.where(col == last, 0.0, pltpu.roll(v, last, 0)).astype(BF16)
        return carry

    lax.fori_loop(0, 24, shift, 0)

    tokens = 2 * 4 * lat.shape[2]
    per_frame = tokens // 2

    def conv(j, lo, hi):
        def step(i, carry):
            dt, dr = i // 3, i % 3
            total = None
            for dc in range(3):
                patch = win[dc, pl.ds(dt, 2), pl.ds(dr, 4)].reshape(tokens, chans)
                tap = w[j, :, :, :, i * 3 + dc].reshape(chans, cols)
                term = jnp.dot(patch, tap, preferred_element_type=F32)
                total = term if total is None else total + term
            acc[...] += total
            return carry

        lax.fori_loop(lo, hi, step, 0)

    lane = lax.broadcasted_iota(jnp.int32, (cols, cols), 0)
    lane2 = lax.broadcasted_iota(jnp.int32, (cols, cols), 1)
    width = chans // GROUPS
    same = (lane // width == lane2 // width).astype(F32)
    count = per_frame * width

    def group_sum(v):
        return jnp.dot(v, same, preferred_element_type=F32, precision=lax.Precision.HIGHEST)

    def finish_chunk(j):
        c = acc[...].astype(BF16).reshape(2, per_frame, cols)
        kv[j, z] = c
        cf = c.astype(F32)
        mean = group_sum(jnp.sum(cf, axis=1)) * (1.0 / count)
        dev = cf - mean[:, None, :]
        st[z, 0:2, j * cols : (j + 1) * cols] = mean
        st[z, 2:4, j * cols : (j + 1) * cols] = group_sum(jnp.sum(dev * dev, axis=1))
        z_step(j, 0)

    for j in range(CHUNKS):
        finish_gather(j)
        if j >= 1:
            z_step(j - 1, 1)
        acc[...] = jnp.zeros_like(acc)
        conv(j, 0, 3)
        if j + 1 < CHUNKS:
            if j >= 1:
                pass
            start_2b(j + 1)
        if j >= 1:
            z_step(j - 1, 2)
        if j + 2 < CHUNKS:
            start_1b(j + 2)
        conv(j, 3, 6)
        if j + 2 < CHUNKS:
            start_2a(j + 2)
        if j + 3 < CHUNKS:
            start_1a(j + 3)
        if j >= 1:
            z_step(j - 1, 3)
        conv(j, 6, 9)
        finish_chunk(j)
        if j >= 1:
            z_step(j - 1, 4)

    last = CHUNKS - 1
    for d in range(1, NZ):
        send(st.at[z], st.at[z], s_send.at[d - 1], s_recv.at[d - 1], tm, zs(d))
    z_step(last, 1)
    for d in range(1, NZ):
        arrived(st.at[zs(-d)], s_recv.at[d - 1])
    for c in locals_[1 + CHUNKS :]:
        c.wait()

    means = st[:, 0:2, :]
    mean = jnp.sum(means, axis=0) * (1.0 / NZ)
    apart = means - mean[None]
    spread = jnp.sum(st[:, 2:4, :], axis=0) + count * jnp.sum(apart * apart, axis=0)
    rstd = lax.rsqrt(spread * (1.0 / (count * NZ)) + EPSILON)

    def whole(zb, f):
        return jnp.concatenate([kv[j, zb, f] for j in range(CHUNKS)], axis=1)

    for f in range(2):
        mf, rf = mean[f : f + 1], rstd[f : f + 1]
        n = ((whole(z, f).astype(F32) - mf) * rf).astype(BF16)
        q = jnp.dot(n, wts[0], preferred_element_type=F32).astype(BF16)
        qk = lax.dot_general(q, wts[1], (((1,), (1,)), ((), ())), preferred_element_type=F32)
        qs = (qk * (rf * (LOG2E * chans ** (-0.5)))).astype(BF16)
        qq[f] = qs
        qb[f] = jnp.sum(qs.astype(F32) * mf, axis=1, keepdims=True)

    def attend(blocks, first=False):
        for f in range(2):
            keys = [whole(zb, f) for zb in blocks]
            keys = keys[0] if len(keys) == 1 else jnp.concatenate(keys, axis=0)
            s = lax.dot_general(qq[f], keys, (((1,), (1,)), ((), ())), preferred_element_type=F32)
            s = s - qb[f]
            top = jnp.max(s, axis=1, keepdims=True)
            if not first:
                top = jnp.maximum(top, mx[f])
            p = jnp.exp2(s - top).astype(BF16)
            total = jnp.sum(p.astype(F32), axis=1, keepdims=True)
            part = jnp.dot(p, keys, preferred_element_type=F32)
            if not first:
                scale = jnp.exp2(mx[f] - top)
                total = total + den[f] * scale
                part = part + num[f] * scale
            mx[f] = top
            den[f] = total
            num[f] = part

    attend([z], True)
    z_step(last, 2)
    attend([zs(-1), zs(1)])
    z_step(last, 3)
    attend([zs(-2), zs(2)])
    z_step(last, 4)
    attend([zs(-3), zs(3)])
    attend([zs(4)])

    for f in range(2):
        mf, rf = mean[f : f + 1], rstd[f : f + 1]
        u = ((num[f] / den[f] - mf) * rf).astype(BF16)
        v = jnp.dot(u, wts[2], preferred_element_type=F32).astype(BF16)
        o = whole(z, f).astype(F32) + jnp.dot(v, wts[3], preferred_element_type=F32)
        out[f] = o.astype(BF16).reshape(out.shape[1:])

    for src, ss in sent:
        copy(src, src, ss, ss, mate, z).wait_send()


def body(latents, conv_weight, query_weight, key_weight, value_weight, out_weight):
    frames, rows_here, columns, chans = latents.shape
    taps, depth, _ = conv_weight.shape
    tokens = frames * rows_here * columns
    cols = chans // CHUNKS
    dma = pltpu.SemaphoreType.DMA
    return pl.pallas_call(
        kernel,
        out_shape=jax.ShapeDtypeStruct(latents.shape, BF16),
        in_specs=[pl.BlockSpec(memory_space=pl.ANY)] * 6,
        out_specs=pl.BlockSpec(memory_space=pltpu.VMEM),
        scratch_shapes=[
            pltpu.VMEM((4, rows_here + 2, columns, chans), BF16),
            pltpu.VMEM((3, 4, rows_here + 2, columns, chans), BF16),
            pltpu.VMEM((CHUNKS, NX, NY, NC, taps, depth, cols), BF16),
            pltpu.VMEM((CHUNKS, NZ, frames, tokens // frames, cols), BF16),
            pltpu.VMEM((tokens, cols), F32),
            pltpu.VMEM((NZ, 8, chans), F32),
            pltpu.VMEM((4, chans, chans), BF16),
            pltpu.VMEM((frames, tokens // frames, chans), BF16),
            pltpu.VMEM((frames, tokens // frames, 1), F32),
            pltpu.VMEM((frames, tokens // frames, 1), F32),
            pltpu.VMEM((frames, tokens // frames, 1), F32),
            pltpu.VMEM((frames, tokens // frames, chans), F32),
            dma((CHUNKS, 4, 4)), dma((CHUNKS, 4, 4)),
            dma((CHUNKS, 8)), dma((CHUNKS, 8)),
            dma((CHUNKS, 4, 2)), dma((CHUNKS, 4, 2)),
            dma((7,)), dma((7,)),
            dma((NZ - 1,)), dma((NZ - 1,)),
            dma((CHUNKS + 5,)),
        ],
        compiler_params=pltpu.CompilerParams(
            collective_id=0, has_side_effects=True, vmem_limit_bytes=60 * 2**20
        ),
    )(latents, conv_weight, query_weight, key_weight, value_weight, out_weight)


def solution(mesh):
    placed = (P("tm", "rows", None, None), P(None, "tm", None), P(), P(), P(), P())
    return jax.shard_map(
        body, mesh=mesh, in_specs=placed, out_specs=P("tm", "rows", None, None), check_vma=False
    )
```

```python
import functools

import jax
import jax.numpy as jnp
from jax import lax
from jax.experimental import pallas as pl
from jax.experimental.pallas import tpu as pltpu
from jax.sharding import PartitionSpec as P

MESH = pl.DeviceIdType.MESH
F32 = jnp.float32
BF16 = jnp.bfloat16

GROUPS = 32
EPSILON = 1e-06
LOG2E = 1.4426950408889634
NX, NY, NC, NZ = 4, 4, 2, 8
TAPS = 27
CHUNKS = 4

UNITS = (
    (0, 18, 9, 4, 2, 3),
    (0, 9, 9, 2, 1, 4),
    (0, 0, 9, 2, 1, 4),
    (1, 0, 27, 14, 5, 7),
    (2, 0, 27, 14, 5, 7),
    (3, 9, 18, 9, 4, 5),
    (3, 0, 9, 4, 2, 3),
)


def parts(u):
    _, t, m, n, up_a, up_b = UNITS[u]
    a = ((t, n), (t, up_a), (t + up_a, n - up_a))
    t, n = t + n, m - n
    return a, ((t, n), (t, up_b), (t + up_b, n - up_b))


def kernel(
    lat, cw, wq, wk, wv, wo, out,
    raw, win, w, kv, acc, st, wts, qq, qb, mx, den, num,
    w_send, w_recv, d_send, d_recv, z_send, z_recv, h_send, h_recv, s_send, s_recv, loc,
):
    tm = lax.axis_index("tm")
    z = lax.axis_index("rows")
    x, y, core = tm // (NY * NC), tm // NC % NY, tm % NC
    mate = tm + 1 - 2 * core
    ntm = NX * NY * NC

    def at(px, py):
        return (px * NY + py) * NC + core

    def xs(d):
        return (x + d + NX) % NX

    def ys(d):
        return (y + d + NY) % NY

    def zs(d):
        return (z + d + NZ) % NZ

    def copy(src, dst, ss, rs, to_tm, to_z):
        return pltpu.make_async_remote_copy(
            src_ref=src, dst_ref=dst, send_sem=ss, recv_sem=rs,
            device_id={"tm": to_tm, "rows": to_z}, device_id_type=MESH,
        )

    sent = []

    def send(src, dst, ss, rs, to_tm, to_z):
        c = copy(src, dst, ss, rs, to_tm, to_z)
        c.start()
        sent.append((src, ss))

    def arrived(ref, rs):
        copy(ref, ref, rs, rs, mate, z).wait_recv()

    chans = lat.shape[3]
    cols = chans // CHUNKS

    locals_ = [pltpu.make_async_copy(lat, raw.at[2:4, 1:5], loc.at[CHUNKS])]
    for j in range(CHUNKS):
        locals_.append(
            pltpu.make_async_copy(cw.at[:, :, j * cols : (j + 1) * cols], w.at[j, x, y, core], loc.at[j])
        )
    for i, m in enumerate((wq, wk, wv, wo)):
        locals_.append(pltpu.make_async_copy(m, wts.at[i], loc.at[CHUNKS + 1 + i]))
    for c in locals_:
        c.start()

    barrier = pltpu.get_barrier_semaphore()
    peers = [(at(xs(1), y), z), (at(xs(-1), y), z), (at(x, ys(1)), z), (at(x, ys(-1)), z)]
    peers += [(mate, z), ((tm + 1) % ntm, z), ((tm + ntm - 1) % ntm, z)]
    peers += [(tm, zs(d)) for d in range(1, NZ)]
    for ptm, pz in peers:
        pl.semaphore_signal(barrier, inc=1, device_id={"tm": ptm, "rows": pz}, device_id_type=MESH)
    pl.semaphore_wait(barrier, len(peers))

    def own(j, part):
        return cw.at[part[0] : part[0] + part[1], :, j * cols : (j + 1) * cols]

    def piece(j, px, py, part):
        return w.at[j, px, py, core, part[0] : part[0] + part[1]]

    def line_x(j, py, part):
        return w.at[j, :, py, core, part[0] : part[0] + part[1]]

    def line_y(j, px, part):
        return w.at[j, px, :, core, part[0] : part[0] + part[1]]

    def sems(u, r):
        return [(w_send.at[u, r, i], w_recv.at[u, r, i]) for i in range(4)]

    def start_1a(u):
        j = UNITS[u][0]
        (a, _, _), (b, _, _) = parts(u)
        s = sems(u, 0)
        send(own(j, a), piece(j, x, y, a), *s[0], at(xs(1), y), z)
        send(own(j, b), piece(j, x, y, b), *s[2], at(x, ys(1)), z)
        send(own(j, a), piece(j, x, y, a), *s[1], at(xs(-1), y), z)
        send(own(j, b), piece(j, x, y, b), *s[3], at(x, ys(-1)), z)

    def start_1b(u):
        j = UNITS[u][0]
        (a, a1, a2), (b, b1, b2) = parts(u)
        r = w_recv
        s = sems(u, 1)
        arrived(piece(j, xs(-1), y, a), r.at[u, 0, 0])
        src = piece(j, xs(-1), y, a1)
        send(src, src, *s[0], at(xs(1), y), z)
        arrived(piece(j, x, ys(-1), b), r.at[u, 0, 2])
        src = piece(j, x, ys(-1), b1)
        send(src, src, *s[2], at(x, ys(1)), z)
        arrived(piece(j, xs(1), y, a), r.at[u, 0, 1])
        src = piece(j, xs(1), y, a2)
        send(src, src, *s[1], at(xs(-1), y), z)
        arrived(piece(j, x, ys(1), b), r.at[u, 0, 3])
        src = piece(j, x, ys(1), b2)
        send(src, src, *s[3], at(x, ys(-1)), z)

    def to_mate(u, i, ref):
        send(ref, ref, d_send.at[u, i], d_recv.at[u, i], mate, z)

    def start_2a(u):
        j = UNITS[u][0]
        (a, a1, a2), (b, b1, b2) = parts(u)
        r = w_recv
        arrived(piece(j, xs(2), y, a1), r.at[u, 1, 0])
        arrived(piece(j, xs(2), y, a2), r.at[u, 1, 1])
        arrived(piece(j, x, ys(2), b1), r.at[u, 1, 2])
        arrived(piece(j, x, ys(2), b2), r.at[u, 1, 3])
        if u == 0 or UNITS[u - 1][0] != j:
            locals_[1 + j].wait()
        for half in range(2):
            s = sems(u, 2 + half)
            up_a, down_a = ((a1, a2), (a2, a1))[half]
            up_b, down_b = ((b1, b2), (b2, b1))[half]
            src = line_y(j, x, up_b)
            send(src, src, *s[2], at(xs(1), y), z)
            src = line_y(j, x, down_b)
            send(src, src, *s[3], at(xs(-1), y), z)
            src = line_x(j, y, up_a)
            send(src, src, *s[0], at(x, ys(1)), z)
            src = line_x(j, y, down_a)
            send(src, src, *s[1], at(x, ys(-1)), z)
        to_mate(u, 0, line_x(j, y, a))
        to_mate(u, 1, line_y(j, x, b))

    def start_2b(u):
        j = UNITS[u][0]
        (a, a1, a2), (b, b1, b2) = parts(u)
        r = w_recv
        s = sems(u, 4)
        src = line_y(j, xs(-1), b1)
        arrived(src, r.at[u, 2, 2])
        send(src, src, *s[2], at(xs(1), y), z)
        src = line_y(j, xs(1), b2)
        arrived(src, r.at[u, 2, 3])
        send(src, src, *s[3], at(xs(-1), y), z)
        src = line_x(j, ys(-1), a1)
        arrived(src, r.at[u, 2, 0])
        send(src, src, *s[0], at(x, ys(1)), z)
        src = line_x(j, ys(1), a2)
        arrived(src, r.at[u, 2, 1])
        send(src, src, *s[1], at(x, ys(-1)), z)

    def near_lines(u):
        j = UNITS[u][0]
        (a, a1, a2), (b, b1, b2) = parts(u)
        r = w_recv
        arrived(line_x(j, ys(-1), a2), r.at[u, 3, 0])
        to_mate(u, 2, line_x(j, ys(-1), a))
        arrived(line_x(j, ys(1), a1), r.at[u, 3, 1])
        to_mate(u, 3, line_x(j, ys(1), a))
        arrived(line_y(j, xs(-1), b2), r.at[u, 3, 2])
        to_mate(u, 4, line_y(j, xs(-1), b))
        arrived(line_y(j, xs(1), b1), r.at[u, 3, 3])
        to_mate(u, 5, line_y(j, xs(1), b))

    def finish_gather(u):
        j = UNITS[u][0]
        (a, a1, a2), (b, b1, b2) = parts(u)
        r = w_recv
        arrived(line_x(j, ys(2), a1), r.at[u, 4, 0])
        arrived(line_x(j, ys(2), a2), r.at[u, 4, 1])
        to_mate(u, 6, line_x(j, ys(2), a))
        arrived(line_y(j, xs(2), b1), r.at[u, 4, 2])
        arrived(line_y(j, xs(2), b2), r.at[u, 4, 3])
        to_mate(u, 7, line_y(j, xs(2), b))
        other = 1 - core
        for i, (d, along_x) in enumerate(
            ((0, True), (0, False), (-1, True), (1, True), (-1, False), (1, False), (2, True), (2, False))
        ):
            if along_x:
                ref = w.at[j, :, ys(d), other, a[0] : a[0] + a[1]]
            else:
                ref = w.at[j, xs(d), :, other, b[0] : b[0] + b[1]]
            arrived(ref, d_recv.at[u, i])

    def z_step(j, r, frames=(0, 1)):
        for f in frames:
            if r == 0:
                low = high = kv.at[j, z, f]
            elif r < 4:
                low, high = kv.at[j, zs(-r), f], kv.at[j, zs(r), f]
                arrived(low, z_recv.at[j, r - 1, 0, f])
                arrived(high, z_recv.at[j, r - 1, 1, f])
            else:
                arrived(kv.at[j, zs(4), f], z_recv.at[j, 3, f, f])
            if r < 3 or (r == 3 and f == 0):
                send(low, low, z_send.at[j, r, 0, f], z_recv.at[j, r, 0, f], tm, zs(1))
            if r < 3 or (r == 3 and f == 1):
                send(high, high, z_send.at[j, r, 1, f], z_recv.at[j, r, 1, f], tm, zs(-1))

    nxt = (tm + 1) % ntm
    start_1a(0)
    send(lat.at[:, 0], raw.at[0:2, 1], h_send.at[0], h_recv.at[0], nxt, z)
    send(lat.at[:, 3], raw.at[0:2, 4], h_send.at[1], h_recv.at[1], nxt, z)
    send(lat.at[:, 0], raw.at[2:4, 5], h_send.at[3], h_recv.at[3], tm, zs(-1))
    send(lat.at[:, 3], raw.at[2:4, 0], h_send.at[4], h_recv.at[4], tm, zs(1))
    start_1a(1)
    acc[...] = jnp.zeros_like(acc)

    col = lax.broadcasted_iota(jnp.int32, (lat.shape[2], chans), 0)

    def shift(i, carry):
        f, r = i // 6, i % 6
        outside = ((r == 0) & (z == 0)) | ((r == 5) & (z == NZ - 1)) | ((f < 2) & (tm == 0))
        keep = jnp.where(outside, 0.0, 1.0).astype(F32)
        v = raw[f, r].astype(F32) * keep
        win[1, f, r] = v.astype(BF16)
        last = lat.shape[2] - 1
        win[0, f, r] = jnp.where(col == 0, 0.0, pltpu.roll(v, 1, 0)).astype(BF16)
        win[2, f, r] = jnp.where(col == last, 0.0, pltpu.roll(v, last, 0)).astype(BF16)
        return carry

    tokens = 2 * 4 * lat.shape[2]
    per_frame = tokens // 2

    def conv(u, lo, hi):
        j, first, count_, *_ = UNITS[u]
        lags = range(first // 9, (first + count_) // 9)

        def step(i, carry):
            dr, dc = i // 3, i % 3
            sums = [None, None]
            for f in range(4):
                pairs = [(g, f - g) for g in range(2) if f - g in lags]
                if not pairs:
                    continue
                patch = win[dc, f, pl.ds(dr, 4)].reshape(per_frame, chans)
                taps = [w[j, :, :, :, 9 * lag + i].reshape(chans, cols) for _, lag in pairs]
                tap = taps[0] if len(taps) == 1 else jnp.concatenate(taps, axis=1)
                term = jnp.dot(patch, tap, preferred_element_type=F32)
                for k, (g, _) in enumerate(pairs):
                    t = term[:, k * cols : (k + 1) * cols]
                    sums[g] = t if sums[g] is None else sums[g] + t
            for g in range(2):
                acc[g] += sums[g]
            return carry

        lax.fori_loop(lo, hi, step, 0)

    lane = lax.broadcasted_iota(jnp.int32, (cols, cols), 0)
    lane2 = lax.broadcasted_iota(jnp.int32, (cols, cols), 1)
    width = chans // GROUPS
    same = (lane // width == lane2 // width).astype(F32)
    count = per_frame * width

    def group_sum(v):
        return jnp.dot(v, same, preferred_element_type=F32, precision=lax.Precision.HIGHEST)

    def finish_chunk(j):
        c = acc[...].astype(BF16)
        acc[...] = jnp.zeros_like(acc)
        kv[j, z] = c
        cf = c.astype(F32)
        mean = group_sum(jnp.sum(cf, axis=1)) * (1.0 / count)
        dev = cf - mean[:, None, :]
        st[z, 0:2, j * cols : (j + 1) * cols] = mean
        st[z, 2:4, j * cols : (j + 1) * cols] = group_sum(jnp.sum(dev * dev, axis=1))
        z_step(j, 0)

    last = CHUNKS - 1
    start_1b(0)
    start_2a(0)
    send(lat.at[:, 1:3], raw.at[0:2, 2:4], h_send.at[2], h_recv.at[2], nxt, z)
    start_1a(2)
    arrived(raw.at[2:4, 5], h_recv.at[3])
    arrived(raw.at[2:4, 0], h_recv.at[4])
    locals_[0].wait()
    arrived(raw.at[0:2, 1], h_recv.at[0])
    send(raw.at[0:2, 1], raw.at[0:2, 5], h_send.at[5], h_recv.at[5], tm, zs(-1))
    arrived(raw.at[0:2, 4], h_recv.at[1])
    send(raw.at[0:2, 4], raw.at[0:2, 0], h_send.at[6], h_recv.at[6], tm, zs(1))
    start_1b(1)
    start_2b(0)
    start_2a(1)
    near_lines(0)
    lax.fori_loop(12, 24, shift, 0)
    start_1b(2)
    start_1a(3)
    finish_gather(0)
    start_2b(1)
    start_2a(2)
    conv(0, 0, 9)
    near_lines(1)
    arrived(raw.at[0:2, 2:4], h_recv.at[2])
    arrived(raw.at[0:2, 5], h_recv.at[5])
    arrived(raw.at[0:2, 0], h_recv.at[6])
    lax.fori_loop(0, 12, shift, 0)
    start_2b(2)
    finish_gather(1)
    start_1b(3)
    conv(1, 0, 9)
    near_lines(2)
    start_2a(3)
    start_1a(4)
    finish_gather(2)
    conv(2, 0, 9)
    finish_chunk(0)
    start_2b(3)
    start_1b(4)
    start_1a(5)
    near_lines(3)
    start_2a(4)
    z_step(0, 1)
    finish_gather(3)
    conv(3, 0, 4)
    start_2b(4)
    start_1b(5)
    start_1a(6)
    z_step(0, 2)
    conv(3, 4, 6)
    near_lines(4)
    start_2a(5)
    conv(3, 6, 9)
    finish_chunk(1)
    z_step(0, 3)
    start_1b(6)
    finish_gather(4)
    conv(4, 0, 2)
    z_step(1, 1)
    start_2b(5)
    conv(4, 2, 6)
    near_lines(5)
    start_2a(6)
    z_step(0, 4)
    conv(4, 6, 9)
    z_step(1, 2)
    finish_chunk(2)
    finish_gather(5)
    start_2b(6)
    conv(5, 0, 9)
    near_lines(6)
    z_step(1, 3)
    z_step(2, 1)
    finish_gather(6)
    conv(6, 0, 9)
    finish_chunk(3)

    for d in range(1, NZ):
        send(st.at[z], st.at[z], s_send.at[d - 1], s_recv.at[d - 1], tm, zs(d))
    z_step(2, 2)
    z_step(last, 1)
    z_step(2, 3)
    z_step(1, 4)
    z_step(2, 4)
    for d in range(1, NZ):
        arrived(st.at[zs(-d)], s_recv.at[d - 1])
    for c in locals_[1 + CHUNKS :]:
        c.wait()

    means = st[:, 0:2, :]
    mean = jnp.sum(means, axis=0) * (1.0 / NZ)
    apart = means - mean[None]
    spread = jnp.sum(st[:, 2:4, :], axis=0) + count * jnp.sum(apart * apart, axis=0)
    rstd = lax.rsqrt(spread * (1.0 / (count * NZ)) + EPSILON)

    def whole(zb, f):
        return jnp.concatenate([kv[j, zb, f] for j in range(CHUNKS)], axis=1)

    for f in range(2):
        mf, rf = mean[f : f + 1], rstd[f : f + 1]
        n = ((whole(z, f).astype(F32) - mf) * rf).astype(BF16)
        q = jnp.dot(n, wts[0], preferred_element_type=F32).astype(BF16)
        qk = lax.dot_general(q, wts[1], (((1,), (1,)), ((), ())), preferred_element_type=F32)
        qs = (qk * (rf * (LOG2E * chans ** (-0.5)))).astype(BF16)
        qq[f] = qs
        qb[f] = jnp.sum(qs.astype(F32) * mf, axis=1, keepdims=True)

    def attend(blocks, first=False):
        for f in range(2):
            keys = [whole(zb, f) for zb in blocks]
            keys = keys[0] if len(keys) == 1 else jnp.concatenate(keys, axis=0)
            s = lax.dot_general(qq[f], keys, (((1,), (1,)), ((), ())), preferred_element_type=F32)
            s = s - qb[f]
            top = jnp.max(s, axis=1, keepdims=True)
            if not first:
                top = jnp.maximum(top, mx[f])
            p = jnp.exp2(s - top).astype(BF16)
            total = jnp.sum(p.astype(F32), axis=1, keepdims=True)
            part = jnp.dot(p, keys, preferred_element_type=F32)
            if not first:
                scale = jnp.exp2(mx[f] - top)
                total = total + den[f] * scale
                part = part + num[f] * scale
            mx[f] = top
            den[f] = total
            num[f] = part

    attend([z], True)
    z_step(last, 2)
    attend([zs(-1), zs(1)])
    z_step(last, 3)
    attend([zs(-2), zs(2)])
    z_step(last, 4)
    attend([zs(-3), zs(3)])
    attend([zs(4)])

    for f in range(2):
        mf, rf = mean[f : f + 1], rstd[f : f + 1]
        u = ((num[f] / den[f] - mf) * rf).astype(BF16)
        v = jnp.dot(u, wts[2], preferred_element_type=F32).astype(BF16)
        o = whole(z, f).astype(F32) + jnp.dot(v, wts[3], preferred_element_type=F32)
        out[f] = o.astype(BF16).reshape(out.shape[1:])

    for src, ss in sent:
        copy(src, src, ss, ss, mate, z).wait_send()


def body(latents, conv_weight, query_weight, key_weight, value_weight, out_weight):
    frames, rows_here, columns, chans = latents.shape
    taps, depth, _ = conv_weight.shape
    tokens = frames * rows_here * columns
    cols = chans // CHUNKS
    dma = pltpu.SemaphoreType.DMA
    return pl.pallas_call(
        kernel,
        out_shape=jax.ShapeDtypeStruct(latents.shape, BF16),
        in_specs=[pl.BlockSpec(memory_space=pl.ANY)] * 6,
        out_specs=pl.BlockSpec(memory_space=pltpu.VMEM),
        scratch_shapes=[
            pltpu.VMEM((4, rows_here + 2, columns, chans), BF16),
            pltpu.VMEM((3, 4, rows_here + 2, columns, chans), BF16),
            pltpu.VMEM((CHUNKS, NX, NY, NC, taps, depth, cols), BF16),
            pltpu.VMEM((CHUNKS, NZ, frames, tokens // frames, cols), BF16),
            pltpu.VMEM((frames, tokens // frames, cols), F32),
            pltpu.VMEM((NZ, 8, chans), F32),
            pltpu.VMEM((4, chans, chans), BF16),
            pltpu.VMEM((frames, tokens // frames, chans), BF16),
            pltpu.VMEM((frames, tokens // frames, 1), F32),
            pltpu.VMEM((frames, tokens // frames, 1), F32),
            pltpu.VMEM((frames, tokens // frames, 1), F32),
            pltpu.VMEM((frames, tokens // frames, chans), F32),
            dma((len(UNITS), 5, 4)), dma((len(UNITS), 5, 4)),
            dma((len(UNITS), 8)), dma((len(UNITS), 8)),
            dma((CHUNKS, 4, 2, 2)), dma((CHUNKS, 4, 2, 2)),
            dma((7,)), dma((7,)),
            dma((NZ - 1,)), dma((NZ - 1,)),
            dma((CHUNKS + 5,)),
        ],
        compiler_params=pltpu.CompilerParams(
            collective_id=0, has_side_effects=True, vmem_limit_bytes=60 * 2**20
        ),
    )(latents, conv_weight, query_weight, key_weight, value_weight, out_weight)


def solution(mesh):
    placed = (P("tm", "rows", None, None), P(None, "tm", None), P(), P(), P(), P())
    return jax.shard_map(
        body, mesh=mesh, in_specs=placed, out_specs=P("tm", "rows", None, None), check_vma=False
    )
```

```python
import functools

import jax
import jax.numpy as jnp
from jax import lax
from jax.experimental import pallas as pl
from jax.experimental.pallas import tpu as pltpu
from jax.sharding import PartitionSpec as P

MESH = pl.DeviceIdType.MESH
F32 = jnp.float32
BF16 = jnp.bfloat16

GROUPS = 32
EPSILON = 1e-06
LOG2E = 1.4426950408889634
NX, NY, NC, NZ = 4, 4, 2, 8
TAPS = 27
CHUNKS = 4

UNITS = (
    (0, 18, 9, 4, 2, 3),
    (0, 0, 18, 4, 1, 7),
    (1, 0, 27, 14, 5, 7),
    (2, 0, 27, 14, 5, 7),
    (3, 9, 18, 9, 4, 5),
    (3, 0, 9, 4, 2, 3),
)


def parts(u):
    _, t, m, n, up_a, up_b = UNITS[u]
    a = ((t, n), (t, up_a), (t + up_a, n - up_a))
    t, n = t + n, m - n
    return a, ((t, n), (t, up_b), (t + up_b, n - up_b))


def kernel(
    lat, cw, wq, wk, wv, wo, out,
    raw, win, w, kv, acc, st, wts, qq, qb, mx, den, num,
    w_send, w_recv, d_send, d_recv, z_send, z_recv, h_send, h_recv, s_send, s_recv, loc,
):
    tm = lax.axis_index("tm")
    z = lax.axis_index("rows")
    x, y, core = tm // (NY * NC), tm // NC % NY, tm % NC
    mate = tm + 1 - 2 * core
    ntm = NX * NY * NC

    def at(px, py):
        return (px * NY + py) * NC + core

    def xs(d):
        return (x + d + NX) % NX

    def ys(d):
        return (y + d + NY) % NY

    def zs(d):
        return (z + d + NZ) % NZ

    def copy(src, dst, ss, rs, to_tm, to_z):
        return pltpu.make_async_remote_copy(
            src_ref=src, dst_ref=dst, send_sem=ss, recv_sem=rs,
            device_id={"tm": to_tm, "rows": to_z}, device_id_type=MESH,
        )

    sent = []

    def send(src, dst, ss, rs, to_tm, to_z):
        c = copy(src, dst, ss, rs, to_tm, to_z)
        c.start()
        sent.append((src, ss))

    def flush():
        for src, ss in sent:
            copy(src, src, ss, ss, mate, z).wait_send()
        sent.clear()

    def arrived(ref, rs):
        copy(ref, ref, rs, rs, mate, z).wait_recv()

    chans = lat.shape[3]
    cols = chans // CHUNKS

    locals_ = [pltpu.make_async_copy(lat, raw.at[2:4, 1:5], loc.at[CHUNKS])]
    for j in range(CHUNKS):
        locals_.append(
            pltpu.make_async_copy(cw.at[:, :, j * cols : (j + 1) * cols], w.at[j, x, y, core], loc.at[j])
        )
    for i, m in enumerate((wq, wk, wv, wo)):
        locals_.append(pltpu.make_async_copy(m, wts.at[i], loc.at[CHUNKS + 1 + i]))
    for i in (1, 0, *range(2, len(locals_))):
        locals_[i].start()

    barrier = pltpu.get_barrier_semaphore()
    peers = [(at(xs(1), y), z), (at(xs(-1), y), z), (at(x, ys(1)), z), (at(x, ys(-1)), z)]
    peers += [(mate, z), ((tm + 1) % ntm, z), ((tm + ntm - 1) % ntm, z)]
    peers += [(tm, zs(d)) for d in range(1, NZ)]
    for ptm, pz in peers:
        pl.semaphore_signal(barrier, inc=1, device_id={"tm": ptm, "rows": pz}, device_id_type=MESH)
    pl.semaphore_wait(barrier, len(peers))

    def piece(j, px, py, part):
        return w.at[j, px, py, core, part[0] : part[0] + part[1]]

    def line_x(j, py, part):
        return w.at[j, :, py, core, part[0] : part[0] + part[1]]

    def line_y(j, px, part):
        return w.at[j, px, :, core, part[0] : part[0] + part[1]]

    def sems(u, r):
        return [(w_send.at[u, r, i], w_recv.at[u, r, i]) for i in range(4)]

    def start_1a(u):
        j = UNITS[u][0]
        (a, _, _), (b, _, _) = parts(u)
        s = sems(u, 0)
        if u == 0 or UNITS[u - 1][0] != j:
            locals_[1 + j].wait()
        src = piece(j, x, y, a)
        send(src, src, *s[0], at(xs(1), y), z)
        send(src, src, *s[1], at(xs(-1), y), z)
        src = piece(j, x, y, b)
        send(src, src, *s[2], at(x, ys(1)), z)
        send(src, src, *s[3], at(x, ys(-1)), z)

    def start_1b(u):
        j = UNITS[u][0]
        (a, a1, a2), (b, b1, b2) = parts(u)
        r = w_recv
        s = sems(u, 1)
        arrived(piece(j, xs(-1), y, a), r.at[u, 0, 0])
        src = piece(j, xs(-1), y, a1)
        send(src, src, *s[0], at(xs(1), y), z)
        arrived(piece(j, x, ys(-1), b), r.at[u, 0, 2])
        src = piece(j, x, ys(-1), b1)
        send(src, src, *s[2], at(x, ys(1)), z)
        arrived(piece(j, xs(1), y, a), r.at[u, 0, 1])
        src = piece(j, xs(1), y, a2)
        send(src, src, *s[1], at(xs(-1), y), z)
        arrived(piece(j, x, ys(1), b), r.at[u, 0, 3])
        src = piece(j, x, ys(1), b2)
        send(src, src, *s[3], at(x, ys(-1)), z)

    def to_mate(u, i, ref):
        send(ref, ref, d_send.at[u, i], d_recv.at[u, i], mate, z)

    def start_2a(u):
        j = UNITS[u][0]
        (a, a1, a2), (b, b1, b2) = parts(u)
        r = w_recv
        arrived(piece(j, xs(2), y, a1), r.at[u, 1, 0])
        arrived(piece(j, xs(2), y, a2), r.at[u, 1, 1])
        arrived(piece(j, x, ys(2), b1), r.at[u, 1, 2])
        arrived(piece(j, x, ys(2), b2), r.at[u, 1, 3])
        for half in range(2):
            s = sems(u, 2 + half)
            up_a, down_a = ((a1, a2), (a2, a1))[half]
            up_b, down_b = ((b1, b2), (b2, b1))[half]
            src = line_y(j, x, up_b)
            send(src, src, *s[2], at(xs(1), y), z)
            src = line_y(j, x, down_b)
            send(src, src, *s[3], at(xs(-1), y), z)
            src = line_x(j, y, up_a)
            send(src, src, *s[0], at(x, ys(1)), z)
            src = line_x(j, y, down_a)
            send(src, src, *s[1], at(x, ys(-1)), z)
        to_mate(u, 0, line_x(j, y, a))
        to_mate(u, 1, line_y(j, x, b))

    def start_2b(u):
        j = UNITS[u][0]
        (a, a1, a2), (b, b1, b2) = parts(u)
        r = w_recv
        s = sems(u, 4)
        src = line_y(j, xs(-1), b1)
        arrived(src, r.at[u, 2, 2])
        send(src, src, *s[2], at(xs(1), y), z)
        src = line_y(j, xs(1), b2)
        arrived(src, r.at[u, 2, 3])
        send(src, src, *s[3], at(xs(-1), y), z)
        src = line_x(j, ys(-1), a1)
        arrived(src, r.at[u, 2, 0])
        send(src, src, *s[0], at(x, ys(1)), z)
        src = line_x(j, ys(1), a2)
        arrived(src, r.at[u, 2, 1])
        send(src, src, *s[1], at(x, ys(-1)), z)

    def near_lines(u):
        j = UNITS[u][0]
        (a, a1, a2), (b, b1, b2) = parts(u)
        r = w_recv
        arrived(line_x(j, ys(-1), a2), r.at[u, 3, 0])
        to_mate(u, 2, line_x(j, ys(-1), a))
        arrived(line_x(j, ys(1), a1), r.at[u, 3, 1])
        to_mate(u, 3, line_x(j, ys(1), a))
        arrived(line_y(j, xs(-1), b2), r.at[u, 3, 2])
        to_mate(u, 4, line_y(j, xs(-1), b))
        arrived(line_y(j, xs(1), b1), r.at[u, 3, 3])
        to_mate(u, 5, line_y(j, xs(1), b))

    def finish_gather(u):
        j = UNITS[u][0]
        (a, a1, a2), (b, b1, b2) = parts(u)
        r = w_recv
        arrived(line_x(j, ys(2), a1), r.at[u, 4, 0])
        arrived(line_x(j, ys(2), a2), r.at[u, 4, 1])
        to_mate(u, 6, line_x(j, ys(2), a))
        arrived(line_y(j, xs(2), b1), r.at[u, 4, 2])
        arrived(line_y(j, xs(2), b2), r.at[u, 4, 3])
        to_mate(u, 7, line_y(j, xs(2), b))
        other = 1 - core
        for i, (d, along_x) in enumerate(
            ((0, True), (0, False), (-1, True), (1, True), (-1, False), (1, False), (2, True), (2, False))
        ):
            if along_x:
                ref = w.at[j, :, ys(d), other, a[0] : a[0] + a[1]]
            else:
                ref = w.at[j, xs(d), :, other, b[0] : b[0] + b[1]]
            arrived(ref, d_recv.at[u, i])

    def z_step(j, r, frames=(0, 1)):
        for f in frames:
            if r == 0:
                low = high = kv.at[j, z, f]
            elif r < 4:
                low, high = kv.at[j, zs(-r), f], kv.at[j, zs(r), f]
                arrived(low, z_recv.at[j, r - 1, 0, f])
                arrived(high, z_recv.at[j, r - 1, 1, f])
            else:
                arrived(kv.at[j, zs(4), f], z_recv.at[j, 3, f, f])
            if r < 3 or (r == 3 and f == 0):
                send(low, low, z_send.at[j, r, 0, f], z_recv.at[j, r, 0, f], tm, zs(1))
            if r < 3 or (r == 3 and f == 1):
                send(high, high, z_send.at[j, r, 1, f], z_recv.at[j, r, 1, f], tm, zs(-1))

    nxt = (tm + 1) % ntm
    start_1a(0)
    start_1a(1)
    send(lat.at[:, 0], raw.at[2:4, 5], h_send.at[3], h_recv.at[3], tm, zs(-1))
    send(lat.at[:, 3], raw.at[2:4, 0], h_send.at[4], h_recv.at[4], tm, zs(1))
    acc[...] = jnp.zeros_like(acc)

    col = lax.broadcasted_iota(jnp.int32, (lat.shape[2], chans), 0)

    def shift(i, carry):
        f, r = i // 6, i % 6
        outside = ((r == 0) & (z == 0)) | ((r == 5) & (z == NZ - 1)) | ((f < 2) & (tm == 0))
        keep = jnp.where(outside, 0.0, 1.0).astype(F32)
        v = raw[f, r].astype(F32) * keep
        win[1, f, r] = v.astype(BF16)
        last = lat.shape[2] - 1
        win[0, f, r] = jnp.where(col == 0, 0.0, pltpu.roll(v, 1, 0)).astype(BF16)
        win[2, f, r] = jnp.where(col == last, 0.0, pltpu.roll(v, last, 0)).astype(BF16)
        return carry

    tokens = 2 * 4 * lat.shape[2]
    per_frame = tokens // 2

    def conv(u, lo, hi):
        j, first, count_, *_ = UNITS[u]
        lags = range(first // 9, (first + count_) // 9)

        def step(i, carry):
            dr, dc = i // 3, i % 3
            sums = [None, None]
            for f in range(4):
                pairs = [(g, f - g) for g in range(2) if f - g in lags]
                if not pairs:
                    continue
                patch = win[dc, f, pl.ds(dr, 4)].reshape(per_frame, chans)
                taps = [w[j, :, :, :, 9 * lag + i].reshape(chans, cols) for _, lag in pairs]
                tap = taps[0] if len(taps) == 1 else jnp.concatenate(taps, axis=1)
                term = jnp.dot(patch, tap, preferred_element_type=F32)
                for k, (g, _) in enumerate(pairs):
                    t = term[:, k * cols : (k + 1) * cols]
                    sums[g] = t if sums[g] is None else sums[g] + t
            for g in range(2):
                acc[g] += sums[g]
            return carry

        lax.fori_loop(lo, hi, step, 0)

    lane = lax.broadcasted_iota(jnp.int32, (cols, cols), 0)
    lane2 = lax.broadcasted_iota(jnp.int32, (cols, cols), 1)
    width = chans // GROUPS
    same = (lane // width == lane2 // width).astype(F32)
    count = per_frame * width

    def group_sum(v):
        return jnp.dot(v, same, preferred_element_type=F32, precision=lax.Precision.HIGHEST)

    def finish_chunk(j):
        c = acc[...].astype(BF16)
        acc[...] = jnp.zeros_like(acc)
        kv[j, z] = c
        cf = c.astype(F32)
        mean = group_sum(jnp.sum(cf, axis=1)) * (1.0 / count)
        dev = cf - mean[:, None, :]
        st[z, 0:2, j * cols : (j + 1) * cols] = mean
        st[z, 2:4, j * cols : (j + 1) * cols] = group_sum(jnp.sum(dev * dev, axis=1))
        z_step(j, 0)

    last = CHUNKS - 1

    def start_group(u):
        if u + 2 < len(UNITS):
            start_1a(u + 2)
        if u + 1 < len(UNITS):
            start_1b(u + 1)
        start_2a(u)

    start_1b(0)
    start_group(0)
    send(lat.at[:, 0], raw.at[0:2, 1], h_send.at[0], h_recv.at[0], nxt, z)
    send(lat.at[:, 3], raw.at[0:2, 4], h_send.at[1], h_recv.at[1], nxt, z)
    arrived(raw.at[2:4, 5], h_recv.at[3])
    arrived(raw.at[2:4, 0], h_recv.at[4])
    locals_[0].wait()
    lax.fori_loop(12, 24, shift, 0)
    start_2b(0)
    send(lat.at[:, 1:3], raw.at[0:2, 2:4], h_send.at[2], h_recv.at[2], nxt, z)
    start_group(1)
    near_lines(0)
    arrived(raw.at[0:2, 1], h_recv.at[0])
    send(raw.at[0:2, 1], raw.at[0:2, 5], h_send.at[5], h_recv.at[5], tm, zs(-1))
    arrived(raw.at[0:2, 4], h_recv.at[1])
    send(raw.at[0:2, 4], raw.at[0:2, 0], h_send.at[6], h_recv.at[6], tm, zs(1))
    finish_gather(0)
    start_2b(1)
    start_group(2)
    conv(0, 0, 9)
    near_lines(1)
    arrived(raw.at[0:2, 2:4], h_recv.at[2])
    arrived(raw.at[0:2, 5], h_recv.at[5])
    arrived(raw.at[0:2, 0], h_recv.at[6])
    lax.fori_loop(0, 12, shift, 0)
    finish_gather(1)
    conv(1, 0, 5)
    start_2b(2)
    start_group(3)
    conv(1, 5, 9)
    finish_chunk(0)
    near_lines(2)
    z_step(0, 1)
    finish_gather(2)
    conv(2, 0, 3)
    start_2b(3)
    start_group(4)
    conv(2, 3, 9)
    z_step(0, 2)
    finish_chunk(1)
    near_lines(3)
    start_2b(4)
    start_group(5)
    z_step(0, 3)
    finish_gather(3)
    z_step(1, 1)
    conv(3, 0, 5)
    near_lines(4)
    start_2b(5)
    conv(3, 5, 9)
    z_step(1, 2)
    finish_chunk(2)
    near_lines(5)
    finish_gather(4)
    conv(4, 0, 9)
    z_step(1, 3)
    z_step(2, 1)
    finish_gather(5)
    conv(5, 0, 9)
    finish_chunk(3)

    for d in range(1, NZ):
        send(st.at[z], st.at[z], s_send.at[d - 1], s_recv.at[d - 1], tm, zs(d))
    z_step(2, 2)
    z_step(last, 1)
    for d in range(1, NZ):
        arrived(st.at[zs(-d)], s_recv.at[d - 1])
    for c in locals_[1 + CHUNKS :]:
        c.wait()

    means = st[:, 0:2, :]
    mean = jnp.sum(means, axis=0) * (1.0 / NZ)
    apart = means - mean[None]
    spread = jnp.sum(st[:, 2:4, :], axis=0) + count * jnp.sum(apart * apart, axis=0)
    rstd = lax.rsqrt(spread * (1.0 / (count * NZ)) + EPSILON)

    def whole(zb, f):
        return jnp.concatenate([kv[j, zb, f] for j in range(CHUNKS)], axis=1)

    for f in range(2):
        mf, rf = mean[f : f + 1], rstd[f : f + 1]
        n = ((whole(z, f).astype(F32) - mf) * rf).astype(BF16)
        q = jnp.dot(n, wts[0], preferred_element_type=F32).astype(BF16)
        qk = lax.dot_general(q, wts[1], (((1,), (1,)), ((), ())), preferred_element_type=F32)
        qs = (qk * (rf * (LOG2E * chans ** (-0.5)))).astype(BF16)
        qq[f] = qs
        qb[f] = jnp.sum(qs.astype(F32) * mf, axis=1, keepdims=True)

    def attend(blocks, first=False):
        for f in range(2):
            keys = [whole(zb, f) for zb in blocks]
            keys = keys[0] if len(keys) == 1 else jnp.concatenate(keys, axis=0)
            s = lax.dot_general(qq[f], keys, (((1,), (1,)), ((), ())), preferred_element_type=F32)
            s = s - qb[f]
            top = jnp.max(s, axis=1, keepdims=True)
            if not first:
                top = jnp.maximum(top, mx[f])
            p = jnp.exp2(s - top).astype(BF16)
            total = jnp.sum(p.astype(F32), axis=1, keepdims=True)
            part = jnp.dot(p, keys, preferred_element_type=F32)
            if not first:
                scale = jnp.exp2(mx[f] - top)
                total = total + den[f] * scale
                part = part + num[f] * scale
            mx[f] = top
            den[f] = total
            num[f] = part

    z_step(2, 3)
    attend([z], True)
    z_step(last, 2)
    attend([zs(-1), zs(1)])
    flush()
    z_step(last, 3)
    attend([zs(-2), zs(2)])
    attend([zs(-3), zs(3)])
    for j in range(CHUNKS):
        z_step(j, 4)
    attend([zs(4)])

    for f in range(2):
        mf, rf = mean[f : f + 1], rstd[f : f + 1]
        u = ((num[f] / den[f] - mf) * rf).astype(BF16)
        v = jnp.dot(u, wts[2], preferred_element_type=F32).astype(BF16)
        o = whole(z, f).astype(F32) + jnp.dot(v, wts[3], preferred_element_type=F32)
        out[f] = o.astype(BF16).reshape(out.shape[1:])

    flush()


def body(latents, conv_weight, query_weight, key_weight, value_weight, out_weight):
    frames, rows_here, columns, chans = latents.shape
    taps, depth, _ = conv_weight.shape
    tokens = frames * rows_here * columns
    cols = chans // CHUNKS
    dma = pltpu.SemaphoreType.DMA
    return pl.pallas_call(
        kernel,
        out_shape=jax.ShapeDtypeStruct(latents.shape, BF16),
        in_specs=[pl.BlockSpec(memory_space=pl.ANY)] * 6,
        out_specs=pl.BlockSpec(memory_space=pltpu.VMEM),
        scratch_shapes=[
            pltpu.VMEM((4, rows_here + 2, columns, chans), BF16),
            pltpu.VMEM((3, 4, rows_here + 2, columns, chans), BF16),
            pltpu.VMEM((CHUNKS, NX, NY, NC, taps, depth, cols), BF16),
            pltpu.VMEM((CHUNKS, NZ, frames, tokens // frames, cols), BF16),
            pltpu.VMEM((frames, tokens // frames, cols), F32),
            pltpu.VMEM((NZ, 8, chans), F32),
            pltpu.VMEM((4, chans, chans), BF16),
            pltpu.VMEM((frames, tokens // frames, chans), BF16),
            pltpu.VMEM((frames, tokens // frames, 1), F32),
            pltpu.VMEM((frames, tokens // frames, 1), F32),
            pltpu.VMEM((frames, tokens // frames, 1), F32),
            pltpu.VMEM((frames, tokens // frames, chans), F32),
            dma((len(UNITS), 5, 4)), dma((len(UNITS), 5, 4)),
            dma((len(UNITS), 8)), dma((len(UNITS), 8)),
            dma((CHUNKS, 4, 2, 2)), dma((CHUNKS, 4, 2, 2)),
            dma((7,)), dma((7,)),
            dma((NZ - 1,)), dma((NZ - 1,)),
            dma((CHUNKS + 5,)),
        ],
        compiler_params=pltpu.CompilerParams(
            collective_id=0, has_side_effects=True, vmem_limit_bytes=60 * 2**20
        ),
    )(latents, conv_weight, query_weight, key_weight, value_weight, out_weight)


def solution(mesh):
    placed = (P("tm", "rows", None, None), P(None, "tm", None), P(), P(), P(), P())
    return jax.shard_map(
        body, mesh=mesh, in_specs=placed, out_specs=P("tm", "rows", None, None), check_vma=False
    )
```

```python
import functools

import jax
import jax.numpy as jnp
from jax import lax
from jax.experimental import pallas as pl
from jax.experimental.pallas import tpu as pltpu
from jax.sharding import PartitionSpec as P

MESH = pl.DeviceIdType.MESH
F32 = jnp.float32
BF16 = jnp.bfloat16

GROUPS = 32
EPSILON = 1e-06
LOG2E = 1.4426950408889634
NX, NY, NC, NZ = 4, 4, 2, 8
TAPS = 27
CHUNKS = 4

UNITS = (
    (0, 0, 27, 14, 4, 4),
    (1, 0, 27, 14, 5, 7),
    (2, 0, 27, 14, 5, 7),
    (3, 9, 18, 9, 4, 5),
    (3, 0, 9, 4, 2, 3),
)


def parts(u):
    _, t, m, n, up_a, up_b = UNITS[u]
    a = ((t, n), (t, up_a), (t + up_a, n - up_a))
    t, n = t + n, m - n
    return a, ((t, n), (t, up_b), (t + up_b, n - up_b))


def kernel(
    lat, cw, wq, wk, wv, wo, out,
    raw, win, w, kv, acc, st, wts, qq, qb, mx, den, num,
    w_send, w_recv, z_send, z_recv, h_send, h_recv, s_send, s_recv, loc,
):
    tm = lax.axis_index("tm")
    z = lax.axis_index("rows")
    x, y, core = tm // (NY * NC), tm // NC % NY, tm % NC
    mate = tm + 1 - 2 * core
    ntm = NX * NY * NC

    def at(px, py):
        return (px * NY + py) * NC + core

    def xs(d):
        return (x + d + NX) % NX

    def ys(d):
        return (y + d + NY) % NY

    def zs(d):
        return (z + d + NZ) % NZ

    def copy(src, dst, ss, rs, to_tm, to_z):
        return pltpu.make_async_remote_copy(
            src_ref=src, dst_ref=dst, send_sem=ss, recv_sem=rs,
            device_id={"tm": to_tm, "rows": to_z}, device_id_type=MESH,
        )

    pending = []

    def send(src, dst, ss, rs, to_tm, to_z):
        copy(src, dst, ss, rs, to_tm, to_z).start()

    def flush():
        for ref, ss in pending:
            copy(ref, ref, ss, ss, mate, z).wait_send()
        pending.clear()

    def arrived(ref, rs):
        copy(ref, ref, rs, rs, mate, z).wait_recv()

    chans = lat.shape[3]
    cols = chans // CHUNKS

    locals_ = [pltpu.make_async_copy(lat, raw.at[2:4, 1:5], loc.at[CHUNKS])]
    for j in range(CHUNKS):
        locals_.append(
            pltpu.make_async_copy(cw.at[:, :, j * cols : (j + 1) * cols], w.at[j, x, y, core], loc.at[j])
        )
    for i, m in enumerate((wq, wk, wv, wo)):
        locals_.append(pltpu.make_async_copy(m, wts.at[i], loc.at[CHUNKS + 1 + i]))
    for i in (1, 0, *range(2, len(locals_))):
        locals_[i].start()

    barrier = pltpu.get_barrier_semaphore()
    peers = [(at(xs(d), y), z) for d in range(1, NX)] + [(at(x, ys(d)), z) for d in range(1, NY)]
    peers += [(mate, z), ((tm + 1) % ntm, z), ((tm + ntm - 1) % ntm, z)]
    peers += [(tm, zs(d)) for d in range(1, NZ)]
    for ptm, pz in peers:
        pl.semaphore_signal(barrier, inc=1, device_id={"tm": ptm, "rows": pz}, device_id_type=MESH)
    pl.semaphore_wait(barrier, len(peers))

    def piece(j, px, py, part):
        return w.at[j, px, py, core, part[0] : part[0] + part[1]]

    def line_x(j, py, part):
        return w.at[j, :, py, core, part[0] : part[0] + part[1]]

    def line_y(j, px, part):
        return w.at[j, px, :, core, part[0] : part[0] + part[1]]

    def block(u, *lead):
        j, t, m, *_ = UNITS[u]
        return w.at[(j, *lead, core, slice(t, t + m))]

    everything = slice(None)
    sizes = (0, slice(0, 2)), (0, 0), (slice(0, 2), everything), (0, everything), (everything, everything)

    def sems(u, r, base):
        pending.append((block(u, *sizes[r]), w_send.at[u, r]))
        return [(w_send.at[u, r], w_recv.at[u, base + i]) for i in range(4)]

    def start_1a(u):
        j = UNITS[u][0]
        (a, _, _), (b, _, _) = parts(u)
        s = sems(u, 0, 0)
        if UNITS[u - 1][0] != j:
            locals_[1 + j].wait()
        src = piece(j, x, y, a)
        send(src, src, *s[0], at(xs(1), y), z)
        send(src, src, *s[1], at(xs(-1), y), z)
        src = piece(j, x, y, b)
        send(src, src, *s[2], at(x, ys(1)), z)
        send(src, src, *s[3], at(x, ys(-1)), z)
        if u == 0:
            s = sems(u, 1, 4)
            send(src, src, *s[1], at(x, ys(2)), z)
            src = piece(j, x, y, a)
            send(src, src, *s[0], at(xs(2), y), z)

    def from_mate(u):
        j, t, m, *_ = UNITS[u]
        arrived(w.at[j, :, :, 1 - core, t : t + m], w_recv.at[u, 16])

    def to_mate(u, ref):
        send(ref, ref, w_send.at[u, 4], w_recv.at[u, 16], mate, z)

    def start_1b(u):
        j = UNITS[u][0]
        (a, a1, a2), (b, b1, b2) = parts(u)
        r = w_recv
        s = sems(u, 1, 4)
        arrived(piece(j, xs(-1), y, a), r.at[u, 0])
        src = piece(j, xs(-1), y, a1)
        send(src, src, *s[0], at(xs(1), y), z)
        arrived(piece(j, x, ys(-1), b), r.at[u, 2])
        src = piece(j, x, ys(-1), b1)
        send(src, src, *s[1], at(x, ys(1)), z)
        arrived(piece(j, xs(1), y, a), r.at[u, 1])
        src = piece(j, xs(1), y, a2)
        send(src, src, *s[0], at(xs(-1), y), z)
        arrived(piece(j, x, ys(1), b), r.at[u, 3])
        src = piece(j, x, ys(1), b2)
        send(src, src, *s[1], at(x, ys(-1)), z)

    def start_2a(u):
        j = UNITS[u][0]
        (a, a1, a2), (b, b1, b2) = parts(u)
        r = w_recv
        if u == 0:
            for i, d in enumerate((-1, 1)):
                arrived(piece(j, xs(d), y, a), r.at[u, i])
                arrived(piece(j, x, ys(d), b), r.at[u, 2 + i])
        arrived(piece(j, xs(2), y, a), r.at[u, 4])
        arrived(piece(j, x, ys(2), b), r.at[u, 5])
        for half in range(2):
            s = [(w_send.at[u, 2], w_recv.at[u, 6 + 4 * half + i]) for i in range(4)]
            up_a, down_a = ((a1, a2), (a2, a1))[half]
            up_b, down_b = ((b1, b2), (b2, b1))[half]
            src = line_y(j, x, up_b)
            send(src, src, *s[2], at(xs(1), y), z)
            src = line_y(j, x, down_b)
            send(src, src, *s[3], at(xs(-1), y), z)
            src = line_x(j, y, up_a)
            send(src, src, *s[0], at(x, ys(1)), z)
            src = line_x(j, y, down_a)
            send(src, src, *s[1], at(x, ys(-1)), z)
        pending.append((block(u, *sizes[2]), w_send.at[u, 2]))
        pending.append((block(u, *sizes[4]), w_send.at[u, 4]))
        to_mate(u, line_x(j, y, a))
        to_mate(u, line_y(j, x, b))

    def start_2b(u):
        j = UNITS[u][0]
        (a, a1, a2), (b, b1, b2) = parts(u)
        r = w_recv
        s = sems(u, 3, 14)
        src = line_y(j, xs(-1), b1)
        arrived(src, r.at[u, 8])
        send(src, src, *s[1], at(xs(1), y), z)
        src = line_y(j, xs(1), b2)
        arrived(src, r.at[u, 9])
        send(src, src, *s[1], at(xs(-1), y), z)
        src = line_x(j, ys(-1), a1)
        arrived(src, r.at[u, 6])
        send(src, src, *s[0], at(x, ys(1)), z)
        src = line_x(j, ys(1), a2)
        arrived(src, r.at[u, 7])
        send(src, src, *s[0], at(x, ys(-1)), z)

    def near_lines(u):
        j = UNITS[u][0]
        (a, a1, a2), (b, b1, b2) = parts(u)
        r = w_recv
        arrived(line_x(j, ys(-1), a2), r.at[u, 10])
        to_mate(u, line_x(j, ys(-1), a))
        arrived(line_x(j, ys(1), a1), r.at[u, 11])
        to_mate(u, line_x(j, ys(1), a))
        arrived(line_y(j, xs(-1), b2), r.at[u, 12])
        to_mate(u, line_y(j, xs(-1), b))
        arrived(line_y(j, xs(1), b1), r.at[u, 13])
        to_mate(u, line_y(j, xs(1), b))

    def finish_gather(u):
        j = UNITS[u][0]
        (a, a1, a2), (b, b1, b2) = parts(u)
        arrived(line_x(j, ys(2), a), w_recv.at[u, 14])
        to_mate(u, line_x(j, ys(2), a))
        arrived(line_y(j, xs(2), b), w_recv.at[u, 15])
        to_mate(u, line_y(j, xs(2), b))
        from_mate(u)

    def z_step(j, r, frames=(0, 1)):
        if r == 3:
            pending.append((kv.at[j, 0 : NZ - 1], z_send.at[j]))
        for f in frames:
            if r == 0:
                low = high = kv.at[j, z, f]
            elif r < 4:
                low, high = kv.at[j, zs(-r), f], kv.at[j, zs(r), f]
                arrived(low, z_recv.at[j, r - 1, 0, f])
                arrived(high, z_recv.at[j, r - 1, 1, f])
            else:
                arrived(kv.at[j, zs(4), f], z_recv.at[j, 3, f, f])
            if r < 3 or (r == 3 and f == 0):
                send(low, low, z_send.at[j], z_recv.at[j, r, 0, f], tm, zs(1))
            if r < 3 or (r == 3 and f == 1):
                send(high, high, z_send.at[j], z_recv.at[j, r, 1, f], tm, zs(-1))

    nxt = (tm + 1) % ntm
    start_1a(0)
    send(lat.at[:, 0], raw.at[2:4, 5], h_send.at[3], h_recv.at[3], tm, zs(-1))
    send(lat.at[:, 3], raw.at[2:4, 0], h_send.at[4], h_recv.at[4], tm, zs(1))
    send(lat.at[:, 0], raw.at[0:2, 1], h_send.at[0], h_recv.at[0], nxt, z)
    send(lat.at[:, 3], raw.at[0:2, 4], h_send.at[1], h_recv.at[1], nxt, z)
    send(lat.at[:, 1:3], raw.at[0:2, 2:4], h_send.at[2], h_recv.at[2], nxt, z)
    start_1a(1)
    acc[...] = jnp.zeros_like(acc)

    col = lax.broadcasted_iota(jnp.int32, (lat.shape[2], chans), 0)

    def shift(i, carry):
        f, r = i // 6, i % 6
        outside = ((r == 0) & (z == 0)) | ((r == 5) & (z == NZ - 1)) | ((f < 2) & (tm == 0))
        keep = jnp.where(outside, 0.0, 1.0).astype(F32)
        v = raw[f, r].astype(F32) * keep
        win[1, f, r] = v.astype(BF16)
        last = lat.shape[2] - 1
        win[0, f, r] = jnp.where(col == 0, 0.0, pltpu.roll(v, 1, 0)).astype(BF16)
        win[2, f, r] = jnp.where(col == last, 0.0, pltpu.roll(v, last, 0)).astype(BF16)
        return carry

    tokens = 2 * 4 * lat.shape[2]
    per_frame = tokens // 2

    def conv(u, lo, hi):
        j, first, count_, *_ = UNITS[u]
        lags = range(first // 9, (first + count_) // 9)

        def step(i, carry):
            dr, dc = i // 3, i % 3
            sums = [None, None]
            for f in range(4):
                pairs = [(g, f - g) for g in range(2) if f - g in lags]
                if not pairs:
                    continue
                patch = win[dc, f, pl.ds(dr, 4)].reshape(per_frame, chans)
                taps = [w[j, :, :, :, 9 * lag + i].reshape(chans, cols) for _, lag in pairs]
                tap = taps[0] if len(taps) == 1 else jnp.concatenate(taps, axis=1)
                term = jnp.dot(patch, tap, preferred_element_type=F32)
                for k, (g, _) in enumerate(pairs):
                    t = term[:, k * cols : (k + 1) * cols]
                    sums[g] = t if sums[g] is None else sums[g] + t
            for g in range(2):
                acc[g] += sums[g]
            return carry

        lax.fori_loop(lo, hi, step, 0)

    lane = lax.broadcasted_iota(jnp.int32, (cols, cols), 0)
    lane2 = lax.broadcasted_iota(jnp.int32, (cols, cols), 1)
    width = chans // GROUPS
    same = (lane // width == lane2 // width).astype(F32)
    count = per_frame * width

    def group_sum(v):
        return jnp.dot(v, same, preferred_element_type=F32, precision=lax.Precision.HIGHEST)

    def finish_chunk(j):
        c = acc[...].astype(BF16)
        acc[...] = jnp.zeros_like(acc)
        kv[j, z] = c
        cf = c.astype(F32)
        mean = group_sum(jnp.sum(cf, axis=1)) * (1.0 / count)
        dev = cf - mean[:, None, :]
        st[z, 0:2, j * cols : (j + 1) * cols] = mean
        st[z, 2:4, j * cols : (j + 1) * cols] = group_sum(jnp.sum(dev * dev, axis=1))
        z_step(j, 0)

    last = CHUNKS - 1
    start_2a(0)
    arrived(raw.at[2:4, 5], h_recv.at[3])
    arrived(raw.at[2:4, 0], h_recv.at[4])
    locals_[0].wait()
    lax.fori_loop(12, 24, shift, 0)
    arrived(raw.at[0:2, 1], h_recv.at[0])
    send(raw.at[0:2, 1], raw.at[0:2, 5], h_send.at[5], h_recv.at[5], tm, zs(-1))
    arrived(raw.at[0:2, 4], h_recv.at[1])
    send(raw.at[0:2, 4], raw.at[0:2, 0], h_send.at[6], h_recv.at[6], tm, zs(1))
    start_1b(1)
    start_1a(2)
    start_2b(0)
    start_2a(1)
    near_lines(0)
    start_1b(2)
    start_1a(3)
    arrived(raw.at[0:2, 5], h_recv.at[5])
    arrived(raw.at[0:2, 0], h_recv.at[6])
    arrived(raw.at[0:2, 2:4], h_recv.at[2])
    lax.fori_loop(0, 12, shift, 0)
    pending.extend((raw.at[0:2, 0], h_send.at[i]) for i in (0, 1, 3, 4, 5, 6))
    pending.append((raw.at[0:2, 0:2], h_send.at[2]))
    finish_gather(0)
    start_2b(1)
    start_2a(2)
    start_1b(3)
    start_1a(4)
    conv(0, 0, 9)
    finish_chunk(0)
    near_lines(1)
    start_1b(4)
    finish_gather(1)
    start_2b(2)
    start_2a(3)
    z_step(0, 1)
    conv(1, 0, 6)
    near_lines(2)
    start_2a(4)
    conv(1, 6, 9)
    z_step(0, 2)
    finish_chunk(1)
    start_2b(3)
    finish_gather(2)
    z_step(0, 3)
    z_step(1, 1)
    conv(2, 0, 5)
    near_lines(3)
    start_2b(4)
    conv(2, 5, 9)
    z_step(1, 2)
    finish_chunk(2)
    finish_gather(3)
    near_lines(4)
    conv(3, 0, 9)
    z_step(1, 3)
    z_step(2, 1)
    finish_gather(4)
    conv(4, 0, 9)
    finish_chunk(3)

    for d in range(1, NZ):
        send(st.at[z], st.at[z], s_send.at[0], s_recv.at[0], tm, zs(d))
    pending.append((st.at[0 : NZ - 1], s_send.at[0]))
    z_step(2, 2)
    z_step(last, 1)
    arrived(st.at[0 : NZ - 1], s_recv.at[0])
    for c in locals_[1 + CHUNKS :]:
        c.wait()

    means = st[:, 0:2, :]
    mean = jnp.sum(means, axis=0) * (1.0 / NZ)
    apart = means - mean[None]
    spread = jnp.sum(st[:, 2:4, :], axis=0) + count * jnp.sum(apart * apart, axis=0)
    rstd = lax.rsqrt(spread * (1.0 / (count * NZ)) + EPSILON)

    def whole(zb, f):
        return jnp.concatenate([kv[j, zb, f] for j in range(CHUNKS)], axis=1)

    for f in range(2):
        mf, rf = mean[f : f + 1], rstd[f : f + 1]
        n = ((whole(z, f).astype(F32) - mf) * rf).astype(BF16)
        q = jnp.dot(n, wts[0], preferred_element_type=F32).astype(BF16)
        qk = lax.dot_general(q, wts[1], (((1,), (1,)), ((), ())), preferred_element_type=F32)
        qs = (qk * (rf * (LOG2E * chans ** (-0.5)))).astype(BF16)
        qq[f] = qs
        qb[f] = jnp.sum(qs.astype(F32) * mf, axis=1, keepdims=True)

    def attend(blocks, first=False):
        for f in range(2):
            keys = [whole(zb, f) for zb in blocks]
            keys = keys[0] if len(keys) == 1 else jnp.concatenate(keys, axis=0)
            s = lax.dot_general(qq[f], keys, (((1,), (1,)), ((), ())), preferred_element_type=F32)
            s = s - qb[f]
            top = jnp.max(s, axis=1, keepdims=True)
            if not first:
                top = jnp.maximum(top, mx[f])
            p = jnp.exp2(s - top).astype(BF16)
            total = jnp.sum(p.astype(F32), axis=1, keepdims=True)
            part = jnp.dot(p, keys, preferred_element_type=F32)
            if not first:
                scale = jnp.exp2(mx[f] - top)
                total = total + den[f] * scale
                part = part + num[f] * scale
            mx[f] = top
            den[f] = total
            num[f] = part

    z_step(2, 3)
    attend([z], True)
    z_step(last, 2)
    attend([zs(-1), zs(1)])
    flush()
    z_step(last, 3)
    attend([zs(-2), zs(2)])
    attend([zs(-3), zs(3)])
    for j in range(CHUNKS):
        z_step(j, 4)
    attend([zs(4)])

    for f in range(2):
        mf, rf = mean[f : f + 1], rstd[f : f + 1]
        u = ((num[f] / den[f] - mf) * rf).astype(BF16)
        v = jnp.dot(u, wts[2], preferred_element_type=F32).astype(BF16)
        o = whole(z, f).astype(F32) + jnp.dot(v, wts[3], preferred_element_type=F32)
        out[f] = o.astype(BF16).reshape(out.shape[1:])

    flush()


def body(latents, conv_weight, query_weight, key_weight, value_weight, out_weight):
    frames, rows_here, columns, chans = latents.shape
    taps, depth, _ = conv_weight.shape
    tokens = frames * rows_here * columns
    cols = chans // CHUNKS
    dma = pltpu.SemaphoreType.DMA
    return pl.pallas_call(
        kernel,
        out_shape=jax.ShapeDtypeStruct(latents.shape, BF16),
        in_specs=[pl.BlockSpec(memory_space=pl.ANY)] * 6,
        out_specs=pl.BlockSpec(memory_space=pltpu.VMEM),
        scratch_shapes=[
            pltpu.VMEM((4, rows_here + 2, columns, chans), BF16),
            pltpu.VMEM((3, 4, rows_here + 2, columns, chans), BF16),
            pltpu.VMEM((CHUNKS, NX, NY, NC, taps, depth, cols), BF16),
            pltpu.VMEM((CHUNKS, NZ, frames, tokens // frames, cols), BF16),
            pltpu.VMEM((frames, tokens // frames, cols), F32),
            pltpu.VMEM((NZ, 8, chans), F32),
            pltpu.VMEM((4, chans, chans), BF16),
            pltpu.VMEM((frames, tokens // frames, chans), BF16),
            pltpu.VMEM((frames, tokens // frames, 1), F32),
            pltpu.VMEM((frames, tokens // frames, 1), F32),
            pltpu.VMEM((frames, tokens // frames, 1), F32),
            pltpu.VMEM((frames, tokens // frames, chans), F32),
            dma((len(UNITS), 5)), dma((len(UNITS), 17)),
            dma((CHUNKS,)), dma((CHUNKS, 4, 2, 2)),
            dma((7,)), dma((7,)),
            dma((1,)), dma((1,)),
            dma((CHUNKS + 5,)),
        ],
        compiler_params=pltpu.CompilerParams(
            collective_id=0, has_side_effects=True, vmem_limit_bytes=60 * 2**20
        ),
    )(latents, conv_weight, query_weight, key_weight, value_weight, out_weight)


def solution(mesh):
    placed = (P("tm", "rows", None, None), P(None, "tm", None), P(), P(), P(), P())
    return jax.shard_map(
        body, mesh=mesh, in_specs=placed, out_specs=P("tm", "rows", None, None), check_vma=False
    )
```

```python
import functools

import jax
import jax.numpy as jnp
from jax import lax
from jax.experimental import pallas as pl
from jax.experimental.pallas import tpu as pltpu
from jax.sharding import PartitionSpec as P

MESH = pl.DeviceIdType.MESH
F32 = jnp.float32
BF16 = jnp.bfloat16

GROUPS = 32
EPSILON = 1e-06
LOG2E = 1.4426950408889634
NX, NY, NC, NZ = 4, 4, 2, 8
TAPS = 27
CHUNKS = 4

UNITS = (
    (0, 0, 27, 14, 4, 4),
    (1, 0, 27, 14, 5, 7),
    (2, 0, 27, 14, 5, 7),
    (3, 9, 18, 9, 4, 5),
    (3, 0, 9, 4, 2, 3),
)


def parts(u):
    _, t, m, n, up_a, up_b = UNITS[u]
    a = ((t, n), (t, up_a), (t + up_a, n - up_a))
    t, n = t + n, m - n
    return a, ((t, n), (t, up_b), (t + up_b, n - up_b))


def kernel(
    lat, cw, wq, wk, wv, wo, out,
    raw, win, w, kv, acc, st, wts, qq, qb, mx, den, num,
    w_send, w_recv, z_send, z_recv, h_send, h_recv, s_send, s_recv, loc,
):
    tm = lax.axis_index("tm")
    z = lax.axis_index("rows")
    x, y, core = tm // (NY * NC), tm // NC % NY, tm % NC
    mate = tm + 1 - 2 * core
    ntm = NX * NY * NC

    def at(px, py):
        return (px * NY + py) * NC + core

    def xs(d):
        return (x + d + NX) % NX

    def ys(d):
        return (y + d + NY) % NY

    def zs(d):
        return (z + d + NZ) % NZ

    def copy(src, dst, ss, rs, to_tm, to_z):
        return pltpu.make_async_remote_copy(
            src_ref=src, dst_ref=dst, send_sem=ss, recv_sem=rs,
            device_id={"tm": to_tm, "rows": to_z}, device_id_type=MESH,
        )

    pending = []

    def send(src, dst, ss, rs, to_tm, to_z):
        copy(src, dst, ss, rs, to_tm, to_z).start()

    def flush():
        for ref, ss in pending:
            copy(ref, ref, ss, ss, mate, z).wait_send()
        pending.clear()

    def arrived(ref, rs):
        copy(ref, ref, rs, rs, mate, z).wait_recv()

    chans = lat.shape[3]
    cols = chans // CHUNKS

    locals_ = [pltpu.make_async_copy(lat, raw.at[2:4, 1:5], loc.at[CHUNKS])]
    for j in range(CHUNKS):
        locals_.append(
            pltpu.make_async_copy(cw.at[:, :, j * cols : (j + 1) * cols], w.at[j, x, y, core], loc.at[j])
        )
    for i, m in enumerate((wq, wk, wv, wo)):
        locals_.append(pltpu.make_async_copy(m, wts.at[i], loc.at[CHUNKS + 1 + i]))
    for i in (1, 0, *range(2, len(locals_))):
        locals_[i].start()

    barrier = pltpu.get_barrier_semaphore()
    peers = [(at(xs(d), y), z) for d in range(1, NX)] + [(at(x, ys(d)), z) for d in range(1, NY)]
    peers += [(mate, z), ((tm + 1) % ntm, z), ((tm + ntm - 1) % ntm, z)]
    peers += [(tm, zs(d)) for d in range(1, NZ)]
    for ptm, pz in peers:
        pl.semaphore_signal(barrier, inc=1, device_id={"tm": ptm, "rows": pz}, device_id_type=MESH)
    pl.semaphore_wait(barrier, len(peers))

    def piece(j, px, py, part):
        return w.at[j, px, py, core, part[0] : part[0] + part[1]]

    def line_x(j, py, part):
        return w.at[j, :, py, core, part[0] : part[0] + part[1]]

    def line_y(j, px, part):
        return w.at[j, px, :, core, part[0] : part[0] + part[1]]

    def block(u, *lead):
        j, t, m, *_ = UNITS[u]
        return w.at[(j, *lead, core, slice(t, t + m))]

    everything = slice(None)
    sizes = (0, slice(0, 2)), (0, 0), (slice(0, 2), everything), (0, everything), (everything, everything)

    def sems(u, r, base):
        pending.append((block(u, *sizes[r]), w_send.at[u, r]))
        return [(w_send.at[u, r], w_recv.at[u, base + i]) for i in range(4)]

    def start_1a(u):
        j = UNITS[u][0]
        (a, _, _), (b, _, _) = parts(u)
        s = sems(u, 0, 0)
        if UNITS[u - 1][0] != j:
            locals_[1 + j].wait()
        src = piece(j, x, y, a)
        send(src, src, *s[0], at(xs(1), y), z)
        send(src, src, *s[1], at(xs(-1), y), z)
        src = piece(j, x, y, b)
        send(src, src, *s[2], at(x, ys(1)), z)
        send(src, src, *s[3], at(x, ys(-1)), z)
        if u == 0:
            s = sems(u, 1, 4)
            send(src, src, *s[1], at(x, ys(2)), z)
            src = piece(j, x, y, a)
            send(src, src, *s[0], at(xs(2), y), z)

    def from_mate(u):
        j, t, m, *_ = UNITS[u]
        arrived(w.at[j, :, :, 1 - core, t : t + m], w_recv.at[u, 16])

    def to_mate(u, ref):
        send(ref, ref, w_send.at[u, 4], w_recv.at[u, 16], mate, z)

    def start_1b(u):
        j = UNITS[u][0]
        (a, a1, a2), (b, b1, b2) = parts(u)
        r = w_recv
        s = sems(u, 1, 4)
        arrived(piece(j, xs(-1), y, a), r.at[u, 0])
        src = piece(j, xs(-1), y, a1)
        send(src, src, *s[0], at(xs(1), y), z)
        arrived(piece(j, x, ys(-1), b), r.at[u, 2])
        src = piece(j, x, ys(-1), b1)
        send(src, src, *s[1], at(x, ys(1)), z)
        arrived(piece(j, xs(1), y, a), r.at[u, 1])
        src = piece(j, xs(1), y, a2)
        send(src, src, *s[0], at(xs(-1), y), z)
        arrived(piece(j, x, ys(1), b), r.at[u, 3])
        src = piece(j, x, ys(1), b2)
        send(src, src, *s[1], at(x, ys(-1)), z)

    def start_2a(u):
        j = UNITS[u][0]
        (a, a1, a2), (b, b1, b2) = parts(u)
        r = w_recv
        if u == 0:
            for i, d in enumerate((-1, 1)):
                arrived(piece(j, xs(d), y, a), r.at[u, i])
                arrived(piece(j, x, ys(d), b), r.at[u, 2 + i])
        arrived(piece(j, xs(2), y, a), r.at[u, 4])
        arrived(piece(j, x, ys(2), b), r.at[u, 5])
        for half in range(2):
            s = [(w_send.at[u, 2], w_recv.at[u, 6 + 4 * half + i]) for i in range(4)]
            up_a, down_a = ((a1, a2), (a2, a1))[half]
            up_b, down_b = ((b1, b2), (b2, b1))[half]
            src = line_y(j, x, up_b)
            send(src, src, *s[2], at(xs(1), y), z)
            src = line_y(j, x, down_b)
            send(src, src, *s[3], at(xs(-1), y), z)
            src = line_x(j, y, up_a)
            send(src, src, *s[0], at(x, ys(1)), z)
            src = line_x(j, y, down_a)
            send(src, src, *s[1], at(x, ys(-1)), z)
        pending.append((block(u, *sizes[2]), w_send.at[u, 2]))
        pending.append((block(u, *sizes[4]), w_send.at[u, 4]))
        to_mate(u, line_x(j, y, a))
        to_mate(u, line_y(j, x, b))

    def start_2b(u):
        j = UNITS[u][0]
        (a, a1, a2), (b, b1, b2) = parts(u)
        r = w_recv
        s = sems(u, 3, 14)
        src = line_y(j, xs(-1), b1)
        arrived(src, r.at[u, 8])
        send(src, src, *s[1], at(xs(1), y), z)
        src = line_y(j, xs(1), b2)
        arrived(src, r.at[u, 9])
        send(src, src, *s[1], at(xs(-1), y), z)
        src = line_x(j, ys(-1), a1)
        arrived(src, r.at[u, 6])
        send(src, src, *s[0], at(x, ys(1)), z)
        src = line_x(j, ys(1), a2)
        arrived(src, r.at[u, 7])
        send(src, src, *s[0], at(x, ys(-1)), z)

    def near_lines(u):
        j = UNITS[u][0]
        (a, a1, a2), (b, b1, b2) = parts(u)
        r = w_recv
        arrived(line_x(j, ys(-1), a2), r.at[u, 10])
        to_mate(u, line_x(j, ys(-1), a))
        arrived(line_x(j, ys(1), a1), r.at[u, 11])
        to_mate(u, line_x(j, ys(1), a))
        arrived(line_y(j, xs(-1), b2), r.at[u, 12])
        to_mate(u, line_y(j, xs(-1), b))
        arrived(line_y(j, xs(1), b1), r.at[u, 13])
        to_mate(u, line_y(j, xs(1), b))

    def finish_gather(u):
        j = UNITS[u][0]
        (a, a1, a2), (b, b1, b2) = parts(u)
        arrived(line_x(j, ys(2), a), w_recv.at[u, 14])
        to_mate(u, line_x(j, ys(2), a))
        arrived(line_y(j, xs(2), b), w_recv.at[u, 15])
        to_mate(u, line_y(j, xs(2), b))
        from_mate(u)

    def z_step(j, r, frames=(0, 1)):
        if r == 3:
            pending.append((kv.at[j, 0 : NZ - 1], z_send.at[j]))
        for f in frames:
            if r == 0:
                low = high = kv.at[j, z, f]
            elif r < 4:
                low, high = kv.at[j, zs(-r), f], kv.at[j, zs(r), f]
                arrived(low, z_recv.at[j, r - 1, 0, f])
                arrived(high, z_recv.at[j, r - 1, 1, f])
            else:
                arrived(kv.at[j, zs(4), f], z_recv.at[j, 3, f, f])
            if r < 3 or (r == 3 and f == 0):
                send(low, low, z_send.at[j], z_recv.at[j, r, 0, f], tm, zs(1))
            if r < 3 or (r == 3 and f == 1):
                send(high, high, z_send.at[j], z_recv.at[j, r, 1, f], tm, zs(-1))

    nxt = (tm + 1) % ntm
    start_1a(0)
    send(lat.at[:, 0], raw.at[2:4, 5], h_send.at[3], h_recv.at[3], tm, zs(-1))
    send(lat.at[:, 3], raw.at[2:4, 0], h_send.at[4], h_recv.at[4], tm, zs(1))
    send(lat.at[:, 0], raw.at[0:2, 1], h_send.at[0], h_recv.at[0], nxt, z)
    send(lat.at[:, 3], raw.at[0:2, 4], h_send.at[1], h_recv.at[1], nxt, z)
    send(lat.at[:, 1:3], raw.at[0:2, 2:4], h_send.at[2], h_recv.at[2], nxt, z)
    start_1a(1)
    acc[...] = jnp.zeros_like(acc)

    col = lax.broadcasted_iota(jnp.int32, (lat.shape[2], chans), 0)

    def shift(i, carry):
        f, r = i // 6, i % 6
        outside = ((r == 0) & (z == 0)) | ((r == 5) & (z == NZ - 1)) | ((f < 2) & (tm == 0))
        keep = jnp.where(outside, 0.0, 1.0).astype(F32)
        v = raw[f, r].astype(F32) * keep
        win[1, f, r] = v.astype(BF16)
        last = lat.shape[2] - 1
        win[0, f, r] = jnp.where(col == 0, 0.0, pltpu.roll(v, 1, 0)).astype(BF16)
        win[2, f, r] = jnp.where(col == last, 0.0, pltpu.roll(v, last, 0)).astype(BF16)
        return carry

    tokens = 2 * 4 * lat.shape[2]
    per_frame = tokens // 2

    def conv(u, lo, hi):
        j, first, count_, *_ = UNITS[u]
        lags = range(first // 9, (first + count_) // 9)

        def step(i, carry):
            dr, dc = i // 3, i % 3
            sums = [None, None]
            for f in range(4):
                pairs = [(g, f - g) for g in range(2) if f - g in lags]
                if not pairs:
                    continue
                patch = win[dc, f, pl.ds(dr, 4)].reshape(per_frame, chans)
                taps = [w[j, :, :, :, 9 * lag + i].reshape(chans, cols) for _, lag in pairs]
                tap = taps[0] if len(taps) == 1 else jnp.concatenate(taps, axis=1)
                term = jnp.dot(patch, tap, preferred_element_type=F32)
                for k, (g, _) in enumerate(pairs):
                    t = term[:, k * cols : (k + 1) * cols]
                    sums[g] = t if sums[g] is None else sums[g] + t
            for g in range(2):
                acc[g] += sums[g]
            return carry

        lax.fori_loop(lo, hi, step, 0)

    lane = lax.broadcasted_iota(jnp.int32, (cols, cols), 0)
    lane2 = lax.broadcasted_iota(jnp.int32, (cols, cols), 1)
    width = chans // GROUPS
    same = (lane // width == lane2 // width).astype(F32)
    count = per_frame * width

    def group_sum(v):
        return jnp.dot(v, same, preferred_element_type=F32, precision=lax.Precision.HIGHEST)

    def finish_chunk(j):
        c = acc[...].astype(BF16)
        acc[...] = jnp.zeros_like(acc)
        kv[j, z] = c
        cf = c.astype(F32)
        mean = group_sum(jnp.sum(cf, axis=1)) * (1.0 / count)
        dev = cf - mean[:, None, :]
        st[z, 0:2, j * cols : (j + 1) * cols] = mean
        st[z, 2:4, j * cols : (j + 1) * cols] = group_sum(jnp.sum(dev * dev, axis=1))
        z_step(j, 0)

    last = CHUNKS - 1
    start_2a(0)
    arrived(raw.at[2:4, 5], h_recv.at[3])
    arrived(raw.at[2:4, 0], h_recv.at[4])
    locals_[0].wait()
    lax.fori_loop(12, 24, shift, 0)
    arrived(raw.at[0:2, 1], h_recv.at[0])
    send(raw.at[0:2, 1], raw.at[0:2, 5], h_send.at[5], h_recv.at[5], tm, zs(-1))
    arrived(raw.at[0:2, 4], h_recv.at[1])
    send(raw.at[0:2, 4], raw.at[0:2, 0], h_send.at[6], h_recv.at[6], tm, zs(1))
    start_1b(1)
    start_1a(2)
    start_2b(0)
    start_1a(3)
    near_lines(0)
    arrived(raw.at[0:2, 5], h_recv.at[5])
    arrived(raw.at[0:2, 0], h_recv.at[6])
    arrived(raw.at[0:2, 2:4], h_recv.at[2])
    lax.fori_loop(0, 12, shift, 0)
    pending.extend((raw.at[0:2, 0], h_send.at[i]) for i in (0, 1, 3, 4, 5, 6))
    pending.append((raw.at[0:2, 0:2], h_send.at[2]))
    start_2a(1)
    start_1b(2)
    finish_gather(0)
    conv(0, 0, 2)
    start_2b(1)
    start_1a(4)
    conv(0, 2, 5)
    start_1b(3)
    start_2a(2)
    conv(0, 5, 9)
    finish_chunk(0)
    near_lines(1)
    finish_gather(1)
    conv(1, 0, 2)
    start_2b(2)
    start_1b(4)
    start_2a(3)
    z_step(0, 1)
    conv(1, 2, 6)
    near_lines(2)
    start_2a(4)
    conv(1, 6, 9)
    z_step(0, 2)
    finish_chunk(1)
    start_2b(3)
    finish_gather(2)
    z_step(0, 3)
    z_step(1, 1)
    conv(2, 0, 5)
    near_lines(3)
    start_2b(4)
    conv(2, 5, 9)
    z_step(1, 2)
    finish_chunk(2)
    finish_gather(3)
    near_lines(4)
    conv(3, 0, 9)
    z_step(1, 3)
    z_step(2, 1)
    finish_gather(4)
    conv(4, 0, 9)
    finish_chunk(3)

    for d in range(1, NZ):
        send(st.at[z], st.at[z], s_send.at[0], s_recv.at[0], tm, zs(d))
    pending.append((st.at[0 : NZ - 1], s_send.at[0]))
    z_step(2, 2)
    z_step(last, 1)
    arrived(st.at[0 : NZ - 1], s_recv.at[0])
    for c in locals_[1 + CHUNKS :]:
        c.wait()

    means = st[:, 0:2, :]
    mean = jnp.sum(means, axis=0) * (1.0 / NZ)
    apart = means - mean[None]
    spread = jnp.sum(st[:, 2:4, :], axis=0) + count * jnp.sum(apart * apart, axis=0)
    rstd = lax.rsqrt(spread * (1.0 / (count * NZ)) + EPSILON)

    def whole(zb, f):
        return jnp.concatenate([kv[j, zb, f] for j in range(CHUNKS)], axis=1)

    for f in range(2):
        mf, rf = mean[f : f + 1], rstd[f : f + 1]
        n = ((whole(z, f).astype(F32) - mf) * rf).astype(BF16)
        q = jnp.dot(n, wts[0], preferred_element_type=F32).astype(BF16)
        qk = lax.dot_general(q, wts[1], (((1,), (1,)), ((), ())), preferred_element_type=F32)
        qs = (qk * (rf * (LOG2E * chans ** (-0.5)))).astype(BF16)
        qq[f] = qs
        qb[f] = jnp.sum(qs.astype(F32) * mf, axis=1, keepdims=True)

    def attend(blocks, first=False):
        for f in range(2):
            keys = [whole(zb, f) for zb in blocks]
            keys = keys[0] if len(keys) == 1 else jnp.concatenate(keys, axis=0)
            s = lax.dot_general(qq[f], keys, (((1,), (1,)), ((), ())), preferred_element_type=F32)
            s = s - qb[f]
            top = jnp.max(s, axis=1, keepdims=True)
            if not first:
                top = jnp.maximum(top, mx[f])
            p = jnp.exp2(s - top).astype(BF16)
            total = jnp.sum(p.astype(F32), axis=1, keepdims=True)
            part = jnp.dot(p, keys, preferred_element_type=F32)
            if not first:
                scale = jnp.exp2(mx[f] - top)
                total = total + den[f] * scale
                part = part + num[f] * scale
            mx[f] = top
            den[f] = total
            num[f] = part

    attend([z], True)
    z_step(2, 3)
    attend([zs(-1), zs(1)])
    z_step(last, 2)
    attend([zs(-2), zs(2)])
    flush()
    z_step(last, 3)
    attend([zs(-3), zs(3)])
    for j in range(CHUNKS):
        z_step(j, 4)
    attend([zs(4)])

    for f in range(2):
        mf, rf = mean[f : f + 1], rstd[f : f + 1]
        u = ((num[f] / den[f] - mf) * rf).astype(BF16)
        v = jnp.dot(u, wts[2], preferred_element_type=F32).astype(BF16)
        o = whole(z, f).astype(F32) + jnp.dot(v, wts[3], preferred_element_type=F32)
        out[f] = o.astype(BF16).reshape(out.shape[1:])

    flush()


def body(latents, conv_weight, query_weight, key_weight, value_weight, out_weight):
    frames, rows_here, columns, chans = latents.shape
    taps, depth, _ = conv_weight.shape
    tokens = frames * rows_here * columns
    cols = chans // CHUNKS
    dma = pltpu.SemaphoreType.DMA
    return pl.pallas_call(
        kernel,
        out_shape=jax.ShapeDtypeStruct(latents.shape, BF16),
        in_specs=[pl.BlockSpec(memory_space=pl.ANY)] * 6,
        out_specs=pl.BlockSpec(memory_space=pltpu.VMEM),
        scratch_shapes=[
            pltpu.VMEM((4, rows_here + 2, columns, chans), BF16),
            pltpu.VMEM((3, 4, rows_here + 2, columns, chans), BF16),
            pltpu.VMEM((CHUNKS, NX, NY, NC, taps, depth, cols), BF16),
            pltpu.VMEM((CHUNKS, NZ, frames, tokens // frames, cols), BF16),
            pltpu.VMEM((frames, tokens // frames, cols), F32),
            pltpu.VMEM((NZ, 8, chans), F32),
            pltpu.VMEM((4, chans, chans), BF16),
            pltpu.VMEM((frames, tokens // frames, chans), BF16),
            pltpu.VMEM((frames, tokens // frames, 1), F32),
            pltpu.VMEM((frames, tokens // frames, 1), F32),
            pltpu.VMEM((frames, tokens // frames, 1), F32),
            pltpu.VMEM((frames, tokens // frames, chans), F32),
            dma((len(UNITS), 5)), dma((len(UNITS), 17)),
            dma((CHUNKS,)), dma((CHUNKS, 4, 2, 2)),
            dma((7,)), dma((7,)),
            dma((1,)), dma((1,)),
            dma((CHUNKS + 5,)),
        ],
        compiler_params=pltpu.CompilerParams(
            collective_id=0, has_side_effects=True, vmem_limit_bytes=60 * 2**20
        ),
    )(latents, conv_weight, query_weight, key_weight, value_weight, out_weight)


def solution(mesh):
    placed = (P("tm", "rows", None, None), P(None, "tm", None), P(), P(), P(), P())
    return jax.shard_map(
        body, mesh=mesh, in_specs=placed, out_specs=P("tm", "rows", None, None), check_vma=False
    )
```

```python
import functools

import jax
import jax.numpy as jnp
from jax import lax
from jax.experimental import pallas as pl
from jax.experimental.pallas import tpu as pltpu
from jax.sharding import PartitionSpec as P

MESH = pl.DeviceIdType.MESH
F32 = jnp.float32
BF16 = jnp.bfloat16

GROUPS = 32
EPSILON = 1e-06
LOG2E = 1.4426950408889634
NX, NY, NC, NZ = 4, 4, 2, 8
TAPS = 27
CHUNKS = 4

UNITS = (
    (0, 0, 27, 14, 4, 4),
    (1, 0, 27, 14, 5, 7),
    (2, 0, 27, 14, 5, 7),
    (3, 9, 18, 9, 4, 5),
    (3, 0, 9, 4, 2, 3),
)


def parts(u):
    _, t, m, n, up_a, up_b = UNITS[u]
    a = ((t, n), (t, up_a), (t + up_a, n - up_a))
    t, n = t + n, m - n
    return a, ((t, n), (t, up_b), (t + up_b, n - up_b))


def kernel(
    lat, cw, wq, wk, wv, wo, out,
    raw, win, w, kv, acc, st, wts, qq, qb, mx, den, num,
    w_send, w_recv, z_send, z_recv, h_send, h_recv, s_send, s_recv, loc,
):
    tm = lax.axis_index("tm")
    z = lax.axis_index("rows")
    x, y, core = tm // (NY * NC), tm // NC % NY, tm % NC
    mate = tm + 1 - 2 * core
    ntm = NX * NY * NC

    def at(px, py):
        return (px * NY + py) * NC + core

    def xs(d):
        return (x + d + NX) % NX

    def ys(d):
        return (y + d + NY) % NY

    def zs(d):
        return (z + d + NZ) % NZ

    def copy(src, dst, ss, rs, to_tm, to_z):
        return pltpu.make_async_remote_copy(
            src_ref=src, dst_ref=dst, send_sem=ss, recv_sem=rs,
            device_id={"tm": to_tm, "rows": to_z}, device_id_type=MESH,
        )

    pending = []

    def send(src, dst, ss, rs, to_tm, to_z):
        copy(src, dst, ss, rs, to_tm, to_z).start()

    def flush():
        for ref, ss in pending:
            copy(ref, ref, ss, ss, mate, z).wait_send()
        pending.clear()

    def arrived(ref, rs):
        copy(ref, ref, rs, rs, mate, z).wait_recv()

    chans = lat.shape[3]
    cols = chans // CHUNKS

    locals_ = [pltpu.make_async_copy(lat, raw.at[2:4, 1:5], loc.at[CHUNKS])]
    for j in range(CHUNKS):
        locals_.append(
            pltpu.make_async_copy(cw.at[:, :, j * cols : (j + 1) * cols], w.at[j, x, y, core], loc.at[j])
        )
    for i, m in enumerate((wq, wk, wv, wo)):
        locals_.append(pltpu.make_async_copy(m, wts.at[i], loc.at[CHUNKS + 1 + i]))
    for i in (1, 0, *range(2, len(locals_))):
        locals_[i].start()

    barrier = pltpu.get_barrier_semaphore()
    peers = [(at(xs(d), y), z) for d in range(1, NX)] + [(at(x, ys(d)), z) for d in range(1, NY)]
    peers += [(mate, z), ((tm + 1) % ntm, z), ((tm + ntm - 1) % ntm, z)]
    peers += [(tm, zs(d)) for d in range(1, NZ)]
    for ptm, pz in peers:
        pl.semaphore_signal(barrier, inc=1, device_id={"tm": ptm, "rows": pz}, device_id_type=MESH)
    pl.semaphore_wait(barrier, len(peers))

    def piece(j, px, py, part):
        return w.at[j, px, py, core, part[0] : part[0] + part[1]]

    def line_x(j, py, part):
        return w.at[j, :, py, core, part[0] : part[0] + part[1]]

    def line_y(j, px, part):
        return w.at[j, px, :, core, part[0] : part[0] + part[1]]

    def block(u, *lead):
        j, t, m, *_ = UNITS[u]
        return w.at[(j, *lead, core, slice(t, t + m))]

    everything = slice(None)
    sizes = (0, slice(0, 2)), (0, 0), (slice(0, 2), everything), (0, everything), (everything, everything)

    def sems(u, r, base):
        pending.append((block(u, *sizes[r]), w_send.at[u, r]))
        return [(w_send.at[u, r], w_recv.at[u, base + i]) for i in range(4)]

    def start_1a(u):
        j = UNITS[u][0]
        (a, _, _), (b, _, _) = parts(u)
        s = sems(u, 0, 0)
        if UNITS[u - 1][0] != j:
            locals_[1 + j].wait()
        src = piece(j, x, y, a)
        send(src, src, *s[0], at(xs(1), y), z)
        send(src, src, *s[1], at(xs(-1), y), z)
        src = piece(j, x, y, b)
        send(src, src, *s[2], at(x, ys(1)), z)
        send(src, src, *s[3], at(x, ys(-1)), z)
        if u == 0:
            s = sems(u, 1, 4)
            send(src, src, *s[1], at(x, ys(2)), z)
            src = piece(j, x, y, a)
            send(src, src, *s[0], at(xs(2), y), z)

    def from_mate(u):
        j, t, m, *_ = UNITS[u]
        arrived(w.at[j, :, :, 1 - core, t : t + m], w_recv.at[u, 16])

    def to_mate(u, ref):
        send(ref, ref, w_send.at[u, 4], w_recv.at[u, 16], mate, z)

    def start_1b(u):
        j = UNITS[u][0]
        (a, a1, a2), (b, b1, b2) = parts(u)
        r = w_recv
        s = sems(u, 1, 4)
        arrived(piece(j, xs(-1), y, a), r.at[u, 0])
        src = piece(j, xs(-1), y, a1)
        send(src, src, *s[0], at(xs(1), y), z)
        arrived(piece(j, x, ys(-1), b), r.at[u, 2])
        src = piece(j, x, ys(-1), b1)
        send(src, src, *s[1], at(x, ys(1)), z)
        arrived(piece(j, xs(1), y, a), r.at[u, 1])
        src = piece(j, xs(1), y, a2)
        send(src, src, *s[0], at(xs(-1), y), z)
        arrived(piece(j, x, ys(1), b), r.at[u, 3])
        src = piece(j, x, ys(1), b2)
        send(src, src, *s[1], at(x, ys(-1)), z)

    def start_2a(u):
        j = UNITS[u][0]
        (a, a1, a2), (b, b1, b2) = parts(u)
        r = w_recv
        if u == 0:
            for i, d in enumerate((-1, 1)):
                arrived(piece(j, xs(d), y, a), r.at[u, i])
                arrived(piece(j, x, ys(d), b), r.at[u, 2 + i])
        arrived(piece(j, xs(2), y, a), r.at[u, 4])
        arrived(piece(j, x, ys(2), b), r.at[u, 5])
        for half in range(2):
            s = [(w_send.at[u, 2], w_recv.at[u, 6 + 4 * half + i]) for i in range(4)]
            up_a, down_a = ((a1, a2), (a2, a1))[half]
            up_b, down_b = ((b1, b2), (b2, b1))[half]
            src = line_y(j, x, up_b)
            send(src, src, *s[2], at(xs(1), y), z)
            src = line_y(j, x, down_b)
            send(src, src, *s[3], at(xs(-1), y), z)
            src = line_x(j, y, up_a)
            send(src, src, *s[0], at(x, ys(1)), z)
            src = line_x(j, y, down_a)
            send(src, src, *s[1], at(x, ys(-1)), z)
        pending.append((block(u, *sizes[2]), w_send.at[u, 2]))
        pending.append((block(u, *sizes[4]), w_send.at[u, 4]))
        to_mate(u, line_x(j, y, a))
        to_mate(u, line_y(j, x, b))

    def start_2b(u):
        j = UNITS[u][0]
        (a, a1, a2), (b, b1, b2) = parts(u)
        r = w_recv
        s = sems(u, 3, 14)
        src = line_y(j, xs(-1), b1)
        arrived(src, r.at[u, 8])
        send(src, src, *s[1], at(xs(1), y), z)
        src = line_y(j, xs(1), b2)
        arrived(src, r.at[u, 9])
        send(src, src, *s[1], at(xs(-1), y), z)
        src = line_x(j, ys(-1), a1)
        arrived(src, r.at[u, 6])
        send(src, src, *s[0], at(x, ys(1)), z)
        src = line_x(j, ys(1), a2)
        arrived(src, r.at[u, 7])
        send(src, src, *s[0], at(x, ys(-1)), z)

    def near_lines(u):
        j = UNITS[u][0]
        (a, a1, a2), (b, b1, b2) = parts(u)
        r = w_recv
        arrived(line_x(j, ys(-1), a2), r.at[u, 10])
        to_mate(u, line_x(j, ys(-1), a))
        arrived(line_x(j, ys(1), a1), r.at[u, 11])
        to_mate(u, line_x(j, ys(1), a))
        arrived(line_y(j, xs(-1), b2), r.at[u, 12])
        to_mate(u, line_y(j, xs(-1), b))
        arrived(line_y(j, xs(1), b1), r.at[u, 13])
        to_mate(u, line_y(j, xs(1), b))

    def finish_gather(u):
        j = UNITS[u][0]
        (a, a1, a2), (b, b1, b2) = parts(u)
        arrived(line_x(j, ys(2), a), w_recv.at[u, 14])
        to_mate(u, line_x(j, ys(2), a))
        arrived(line_y(j, xs(2), b), w_recv.at[u, 15])
        to_mate(u, line_y(j, xs(2), b))
        from_mate(u)

    def z_step(j, r, frames=(0, 1)):
        if r == 3:
            pending.append((kv.at[j, 0 : NZ - 1], z_send.at[j]))
        for f in frames:
            if r == 0:
                low = high = kv.at[j, z, f]
            elif r < 4:
                low, high = kv.at[j, zs(-r), f], kv.at[j, zs(r), f]
                arrived(low, z_recv.at[j, r - 1, 0, f])
                arrived(high, z_recv.at[j, r - 1, 1, f])
            else:
                arrived(kv.at[j, zs(4), f], z_recv.at[j, 3, f, f])
            if r < 3 or (r == 3 and f == 0):
                send(low, low, z_send.at[j], z_recv.at[j, r, 0, f], tm, zs(1))
            if r < 3 or (r == 3 and f == 1):
                send(high, high, z_send.at[j], z_recv.at[j, r, 1, f], tm, zs(-1))

    nxt = (tm + 1) % ntm
    start_1a(0)
    send(lat.at[:, 0], raw.at[2:4, 5], h_send.at[3], h_recv.at[3], tm, zs(-1))
    send(lat.at[:, 3], raw.at[2:4, 0], h_send.at[4], h_recv.at[4], tm, zs(1))
    send(lat.at[:, 0], raw.at[0:2, 1], h_send.at[0], h_recv.at[0], nxt, z)
    send(lat.at[:, 3], raw.at[0:2, 4], h_send.at[1], h_recv.at[1], nxt, z)
    send(lat.at[:, 1:3], raw.at[0:2, 2:4], h_send.at[2], h_recv.at[2], nxt, z)
    start_1a(1)
    acc[...] = jnp.zeros_like(acc)

    col = lax.broadcasted_iota(jnp.int32, (lat.shape[2], chans), 0)

    def shift(i, carry):
        f, r = i // 6, i % 6
        outside = ((r == 0) & (z == 0)) | ((r == 5) & (z == NZ - 1)) | ((f < 2) & (tm == 0))
        keep = jnp.where(outside, 0.0, 1.0).astype(F32)
        v = raw[f, r].astype(F32) * keep
        win[1, f, r] = v.astype(BF16)
        last = lat.shape[2] - 1
        win[0, f, r] = jnp.where(col == 0, 0.0, pltpu.roll(v, 1, 0)).astype(BF16)
        win[2, f, r] = jnp.where(col == last, 0.0, pltpu.roll(v, last, 0)).astype(BF16)
        return carry

    tokens = 2 * 4 * lat.shape[2]
    per_frame = tokens // 2

    def conv(u, lo, hi):
        j, first, count_, *_ = UNITS[u]
        lags = range(first // 9, (first + count_) // 9)

        def step(i, carry):
            dr, dc = i // 3, i % 3
            sums = [None, None]
            for f in range(4):
                pairs = [(g, f - g) for g in range(2) if f - g in lags]
                if not pairs:
                    continue
                patch = win[dc, f, pl.ds(dr, 4)].reshape(per_frame, chans)
                taps = [w[j, :, :, :, 9 * lag + i].reshape(chans, cols) for _, lag in pairs]
                tap = taps[0] if len(taps) == 1 else jnp.concatenate(taps, axis=1)
                term = jnp.dot(patch, tap, preferred_element_type=F32)
                for k, (g, _) in enumerate(pairs):
                    t = term[:, k * cols : (k + 1) * cols]
                    sums[g] = t if sums[g] is None else sums[g] + t
            for g in range(2):
                acc[g] += sums[g]
            return carry

        lax.fori_loop(lo, hi, step, 0)

    lane = lax.broadcasted_iota(jnp.int32, (cols, cols), 0)
    lane2 = lax.broadcasted_iota(jnp.int32, (cols, cols), 1)
    width = chans // GROUPS
    same = (lane // width == lane2 // width).astype(F32)
    count = per_frame * width

    def group_sum(v):
        return jnp.dot(v, same, preferred_element_type=F32, precision=lax.Precision.HIGHEST)

    def finish_chunk(j):
        c = acc[...].astype(BF16)
        acc[...] = jnp.zeros_like(acc)
        kv[j, z] = c
        cf = c.astype(F32)
        mean = group_sum(jnp.sum(cf, axis=1)) * (1.0 / count)
        dev = cf - mean[:, None, :]
        st[z, 0:2, j * cols : (j + 1) * cols] = mean
        st[z, 2:4, j * cols : (j + 1) * cols] = group_sum(jnp.sum(dev * dev, axis=1))
        z_step(j, 0)

    last = CHUNKS - 1
    start_2a(0)
    arrived(raw.at[2:4, 5], h_recv.at[3])
    arrived(raw.at[2:4, 0], h_recv.at[4])
    locals_[0].wait()
    lax.fori_loop(12, 24, shift, 0)
    arrived(raw.at[0:2, 1], h_recv.at[0])
    send(raw.at[0:2, 1], raw.at[0:2, 5], h_send.at[5], h_recv.at[5], tm, zs(-1))
    arrived(raw.at[0:2, 4], h_recv.at[1])
    send(raw.at[0:2, 4], raw.at[0:2, 0], h_send.at[6], h_recv.at[6], tm, zs(1))
    start_1b(1)
    start_1a(2)
    start_2b(0)
    start_1a(3)
    near_lines(0)
    arrived(raw.at[0:2, 5], h_recv.at[5])
    arrived(raw.at[0:2, 0], h_recv.at[6])
    arrived(raw.at[0:2, 2:4], h_recv.at[2])
    lax.fori_loop(0, 12, shift, 0)
    pending.extend((raw.at[0:2, 0], h_send.at[i]) for i in (0, 1, 3, 4, 5, 6))
    pending.append((raw.at[0:2, 0:2], h_send.at[2]))
    start_2a(1)
    start_1b(2)
    finish_gather(0)
    conv(0, 0, 2)
    start_2b(1)
    start_1a(4)
    conv(0, 2, 5)
    start_1b(3)
    start_2a(2)
    conv(0, 5, 9)
    finish_chunk(0)
    near_lines(1)
    finish_gather(1)
    conv(1, 0, 2)
    start_2b(2)
    start_1b(4)
    start_2a(3)
    z_step(0, 1)
    conv(1, 2, 6)
    near_lines(2)
    conv(1, 6, 9)
    z_step(0, 2)
    finish_chunk(1)
    start_2b(3)
    finish_gather(2)
    z_step(0, 3)
    start_2a(4)
    z_step(1, 1)
    conv(2, 0, 5)
    near_lines(3)
    start_2b(4)
    conv(2, 5, 9)
    z_step(1, 2)
    finish_chunk(2)
    finish_gather(3)
    near_lines(4)
    conv(3, 0, 9)
    z_step(1, 3)
    z_step(2, 1)
    finish_gather(4)
    conv(4, 0, 9)
    finish_chunk(3)

    for d in range(1, NZ):
        send(st.at[z], st.at[z], s_send.at[0], s_recv.at[0], tm, zs(d))
    pending.append((st.at[0 : NZ - 1], s_send.at[0]))
    z_step(2, 2)
    z_step(last, 1)
    arrived(st.at[0 : NZ - 1], s_recv.at[0])
    for c in locals_[1 + CHUNKS :]:
        c.wait()

    means = st[:, 0:2, :]
    mean = jnp.sum(means, axis=0) * (1.0 / NZ)
    apart = means - mean[None]
    spread = jnp.sum(st[:, 2:4, :], axis=0) + count * jnp.sum(apart * apart, axis=0)
    rstd = lax.rsqrt(spread * (1.0 / (count * NZ)) + EPSILON)

    def whole(zb, f):
        return jnp.concatenate([kv[j, zb, f] for j in range(CHUNKS)], axis=1)

    for f in range(2):
        mf, rf = mean[f : f + 1], rstd[f : f + 1]
        n = ((whole(z, f).astype(F32) - mf) * rf).astype(BF16)
        q = jnp.dot(n, wts[0], preferred_element_type=F32).astype(BF16)
        qk = lax.dot_general(q, wts[1], (((1,), (1,)), ((), ())), preferred_element_type=F32)
        qs = (qk * (rf * (LOG2E * chans ** (-0.5)))).astype(BF16)
        qq[f] = qs
        qb[f] = jnp.sum(qs.astype(F32) * mf, axis=1, keepdims=True)

    def attend(blocks, first=False):
        for f in range(2):
            keys = [whole(zb, f) for zb in blocks]
            keys = keys[0] if len(keys) == 1 else jnp.concatenate(keys, axis=0)
            s = lax.dot_general(qq[f], keys, (((1,), (1,)), ((), ())), preferred_element_type=F32)
            s = s - qb[f]
            top = jnp.max(s, axis=1, keepdims=True)
            if not first:
                top = jnp.maximum(top, mx[f])
            p = jnp.exp2(s - top).astype(BF16)
            total = jnp.sum(p.astype(F32), axis=1, keepdims=True)
            part = jnp.dot(p, keys, preferred_element_type=F32)
            if not first:
                scale = jnp.exp2(mx[f] - top)
                total = total + den[f] * scale
                part = part + num[f] * scale
            mx[f] = top
            den[f] = total
            num[f] = part

    attend([z], True)
    z_step(2, 3)
    attend([zs(-1), zs(1)])
    z_step(last, 2)
    attend([zs(-2), zs(2)])
    flush()
    z_step(last, 3)
    attend([zs(-3), zs(3)])
    for j in range(CHUNKS):
        z_step(j, 4)
    attend([zs(4)])

    for f in range(2):
        mf, rf = mean[f : f + 1], rstd[f : f + 1]
        u = ((num[f] / den[f] - mf) * rf).astype(BF16)
        v = jnp.dot(u, wts[2], preferred_element_type=F32).astype(BF16)
        o = whole(z, f).astype(F32) + jnp.dot(v, wts[3], preferred_element_type=F32)
        out[f] = o.astype(BF16).reshape(out.shape[1:])

    flush()


def body(latents, conv_weight, query_weight, key_weight, value_weight, out_weight):
    frames, rows_here, columns, chans = latents.shape
    taps, depth, _ = conv_weight.shape
    tokens = frames * rows_here * columns
    cols = chans // CHUNKS
    dma = pltpu.SemaphoreType.DMA
    return pl.pallas_call(
        kernel,
        out_shape=jax.ShapeDtypeStruct(latents.shape, BF16),
        in_specs=[pl.BlockSpec(memory_space=pl.ANY)] * 6,
        out_specs=pl.BlockSpec(memory_space=pltpu.VMEM),
        scratch_shapes=[
            pltpu.VMEM((4, rows_here + 2, columns, chans), BF16),
            pltpu.VMEM((3, 4, rows_here + 2, columns, chans), BF16),
            pltpu.VMEM((CHUNKS, NX, NY, NC, taps, depth, cols), BF16),
            pltpu.VMEM((CHUNKS, NZ, frames, tokens // frames, cols), BF16),
            pltpu.VMEM((frames, tokens // frames, cols), F32),
            pltpu.VMEM((NZ, 8, chans), F32),
            pltpu.VMEM((4, chans, chans), BF16),
            pltpu.VMEM((frames, tokens // frames, chans), BF16),
            pltpu.VMEM((frames, tokens // frames, 1), F32),
            pltpu.VMEM((frames, tokens // frames, 1), F32),
            pltpu.VMEM((frames, tokens // frames, 1), F32),
            pltpu.VMEM((frames, tokens // frames, chans), F32),
            dma((len(UNITS), 5)), dma((len(UNITS), 17)),
            dma((CHUNKS,)), dma((CHUNKS, 4, 2, 2)),
            dma((7,)), dma((7,)),
            dma((1,)), dma((1,)),
            dma((CHUNKS + 5,)),
        ],
        compiler_params=pltpu.CompilerParams(
            collective_id=0, has_side_effects=True, vmem_limit_bytes=60 * 2**20
        ),
    )(latents, conv_weight, query_weight, key_weight, value_weight, out_weight)


def solution(mesh):
    placed = (P("tm", "rows", None, None), P(None, "tm", None), P(), P(), P(), P())
    return jax.shard_map(
        body, mesh=mesh, in_specs=placed, out_specs=P("tm", "rows", None, None), check_vma=False
    )
```

```python
import functools

import jax
import jax.numpy as jnp
from jax import lax
from jax.experimental import pallas as pl
from jax.experimental.pallas import tpu as pltpu
from jax.sharding import PartitionSpec as P

MESH = pl.DeviceIdType.MESH
F32 = jnp.float32
BF16 = jnp.bfloat16

GROUPS = 32
EPSILON = 1e-06
LOG2E = 1.4426950408889634
NX, NY, NC, NZ = 4, 4, 2, 8
TAPS = 27
CHUNKS = 4

UNITS = (
    (0, 0, 27, 14, 4, 4),
    (1, 0, 27, 14, 5, 7),
    (2, 0, 27, 14, 5, 7),
    (3, 9, 18, 9, 4, 5),
    (3, 0, 9, 4, 2, 3),
)


def parts(u):
    _, t, m, n, up_a, up_b = UNITS[u]
    a = ((t, n), (t, up_a), (t + up_a, n - up_a))
    t, n = t + n, m - n
    return a, ((t, n), (t, up_b), (t + up_b, n - up_b))


def kernel(
    lat, cw, wq, wk, wv, wo, out,
    raw, win, w, kv, acc, st, wts, qq, qb, mx, den, num,
    w_send, w_recv, z_send, z_recv, h_send, h_recv, s_send, s_recv, loc,
):
    tm = lax.axis_index("tm")
    z = lax.axis_index("rows")
    x, y, core = tm // (NY * NC), tm // NC % NY, tm % NC
    mate = tm + 1 - 2 * core
    ntm = NX * NY * NC

    def at(px, py):
        return (px * NY + py) * NC + core

    def xs(d):
        return (x + d + NX) % NX

    def ys(d):
        return (y + d + NY) % NY

    def zs(d):
        return (z + d + NZ) % NZ

    def copy(src, dst, ss, rs, to_tm, to_z):
        return pltpu.make_async_remote_copy(
            src_ref=src, dst_ref=dst, send_sem=ss, recv_sem=rs,
            device_id={"tm": to_tm, "rows": to_z}, device_id_type=MESH,
        )

    pending = []

    def send(src, dst, ss, rs, to_tm, to_z):
        copy(src, dst, ss, rs, to_tm, to_z).start()

    def flush():
        for ref, ss in pending:
            copy(ref, ref, ss, ss, mate, z).wait_send()
        pending.clear()

    def arrived(ref, rs):
        copy(ref, ref, rs, rs, mate, z).wait_recv()

    chans = lat.shape[3]
    cols = chans // CHUNKS

    locals_ = [pltpu.make_async_copy(lat, raw.at[2:4, 1:5], loc.at[CHUNKS])]
    for j in range(CHUNKS):
        locals_.append(
            pltpu.make_async_copy(cw.at[:, :, j * cols : (j + 1) * cols], w.at[j, x, y, core], loc.at[j])
        )
    for i, m in enumerate((wq, wk, wv, wo)):
        locals_.append(pltpu.make_async_copy(m, wts.at[i], loc.at[CHUNKS + 1 + i]))
    for i in (1, 0, *range(2, len(locals_))):
        locals_[i].start()

    barrier = pltpu.get_barrier_semaphore()
    peers = [(at(xs(d), y), z) for d in range(1, NX)] + [(at(x, ys(d)), z) for d in range(1, NY)]
    peers += [(mate, z), ((tm + 1) % ntm, z), ((tm + ntm - 1) % ntm, z)]
    peers += [(tm, zs(d)) for d in range(1, NZ)]
    for ptm, pz in peers:
        pl.semaphore_signal(barrier, inc=1, device_id={"tm": ptm, "rows": pz}, device_id_type=MESH)
    pl.semaphore_wait(barrier, len(peers))

    def piece(j, px, py, part):
        return w.at[j, px, py, core, part[0] : part[0] + part[1]]

    def line_x(j, py, part):
        return w.at[j, :, py, core, part[0] : part[0] + part[1]]

    def line_y(j, px, part):
        return w.at[j, px, :, core, part[0] : part[0] + part[1]]

    def block(u, *lead):
        j, t, m, *_ = UNITS[u]
        return w.at[(j, *lead, core, slice(t, t + m))]

    everything = slice(None)
    sizes = (0, slice(0, 2)), (0, 0), (slice(0, 2), everything), (0, everything), (everything, everything)

    def sems(u, r, base):
        pending.append((block(u, *sizes[r]), w_send.at[u, r]))
        return [(w_send.at[u, r], w_recv.at[u, base + i]) for i in range(4)]

    def start_1a(u):
        j = UNITS[u][0]
        (a, _, _), (b, _, _) = parts(u)
        s = sems(u, 0, 0)
        if UNITS[u - 1][0] != j:
            locals_[1 + j].wait()
        src = piece(j, x, y, a)
        send(src, src, *s[0], at(xs(1), y), z)
        send(src, src, *s[1], at(xs(-1), y), z)
        src = piece(j, x, y, b)
        send(src, src, *s[2], at(x, ys(1)), z)
        send(src, src, *s[3], at(x, ys(-1)), z)
        if u == 0:
            s = sems(u, 1, 4)
            send(src, src, *s[1], at(x, ys(2)), z)
            src = piece(j, x, y, a)
            send(src, src, *s[0], at(xs(2), y), z)

    def from_mate(u):
        j, t, m, *_ = UNITS[u]
        arrived(w.at[j, :, :, 1 - core, t : t + m], w_recv.at[u, 16])

    def to_mate(u, ref):
        send(ref, ref, w_send.at[u, 4], w_recv.at[u, 16], mate, z)

    def start_1b(u):
        j = UNITS[u][0]
        (a, a1, a2), (b, b1, b2) = parts(u)
        r = w_recv
        s = sems(u, 1, 4)
        arrived(piece(j, xs(-1), y, a), r.at[u, 0])
        src = piece(j, xs(-1), y, a1)
        send(src, src, *s[0], at(xs(1), y), z)
        arrived(piece(j, x, ys(-1), b), r.at[u, 2])
        src = piece(j, x, ys(-1), b1)
        send(src, src, *s[1], at(x, ys(1)), z)
        arrived(piece(j, xs(1), y, a), r.at[u, 1])
        src = piece(j, xs(1), y, a2)
        send(src, src, *s[0], at(xs(-1), y), z)
        arrived(piece(j, x, ys(1), b), r.at[u, 3])
        src = piece(j, x, ys(1), b2)
        send(src, src, *s[1], at(x, ys(-1)), z)

    def start_2a(u):
        j = UNITS[u][0]
        (a, a1, a2), (b, b1, b2) = parts(u)
        r = w_recv
        if u == 0:
            for i, d in enumerate((-1, 1)):
                arrived(piece(j, xs(d), y, a), r.at[u, i])
                arrived(piece(j, x, ys(d), b), r.at[u, 2 + i])
        arrived(piece(j, xs(2), y, a), r.at[u, 4])
        arrived(piece(j, x, ys(2), b), r.at[u, 5])
        for half in range(2):
            s = [(w_send.at[u, 2], w_recv.at[u, 6 + 4 * half + i]) for i in range(4)]
            up_a, down_a = ((a1, a2), (a2, a1))[half]
            up_b, down_b = ((b1, b2), (b2, b1))[half]
            src = line_y(j, x, up_b)
            send(src, src, *s[2], at(xs(1), y), z)
            src = line_y(j, x, down_b)
            send(src, src, *s[3], at(xs(-1), y), z)
            src = line_x(j, y, up_a)
            send(src, src, *s[0], at(x, ys(1)), z)
            src = line_x(j, y, down_a)
            send(src, src, *s[1], at(x, ys(-1)), z)
        pending.append((block(u, *sizes[2]), w_send.at[u, 2]))
        pending.append((block(u, *sizes[4]), w_send.at[u, 4]))
        to_mate(u, line_x(j, y, a))
        to_mate(u, line_y(j, x, b))

    def start_2b(u):
        j = UNITS[u][0]
        (a, a1, a2), (b, b1, b2) = parts(u)
        r = w_recv
        s = sems(u, 3, 14)
        src = line_y(j, xs(-1), b1)
        arrived(src, r.at[u, 8])
        send(src, src, *s[1], at(xs(1), y), z)
        src = line_y(j, xs(1), b2)
        arrived(src, r.at[u, 9])
        send(src, src, *s[1], at(xs(-1), y), z)
        src = line_x(j, ys(-1), a1)
        arrived(src, r.at[u, 6])
        send(src, src, *s[0], at(x, ys(1)), z)
        src = line_x(j, ys(1), a2)
        arrived(src, r.at[u, 7])
        send(src, src, *s[0], at(x, ys(-1)), z)

    def near_lines(u):
        j = UNITS[u][0]
        (a, a1, a2), (b, b1, b2) = parts(u)
        r = w_recv
        arrived(line_x(j, ys(-1), a2), r.at[u, 10])
        to_mate(u, line_x(j, ys(-1), a))
        arrived(line_x(j, ys(1), a1), r.at[u, 11])
        to_mate(u, line_x(j, ys(1), a))
        arrived(line_y(j, xs(-1), b2), r.at[u, 12])
        to_mate(u, line_y(j, xs(-1), b))
        arrived(line_y(j, xs(1), b1), r.at[u, 13])
        to_mate(u, line_y(j, xs(1), b))

    def finish_gather(u):
        j = UNITS[u][0]
        (a, a1, a2), (b, b1, b2) = parts(u)
        arrived(line_x(j, ys(2), a), w_recv.at[u, 14])
        to_mate(u, line_x(j, ys(2), a))
        arrived(line_y(j, xs(2), b), w_recv.at[u, 15])
        to_mate(u, line_y(j, xs(2), b))
        from_mate(u)

    def z_step(j, r, frames=(0, 1)):
        if r == 3:
            pending.append((kv.at[j, 0 : NZ - 1], z_send.at[j]))
        for f in frames:
            if r == 0:
                low = high = kv.at[j, z, f]
            elif r < 4:
                low, high = kv.at[j, zs(-r), f], kv.at[j, zs(r), f]
                arrived(low, z_recv.at[j, r - 1, 0, f])
                arrived(high, z_recv.at[j, r - 1, 1, f])
            else:
                arrived(kv.at[j, zs(4), f], z_recv.at[j, 3, f, f])
            if r < 3 or (r == 3 and f == 0):
                send(low, low, z_send.at[j], z_recv.at[j, r, 0, f], tm, zs(1))
            if r < 3 or (r == 3 and f == 1):
                send(high, high, z_send.at[j], z_recv.at[j, r, 1, f], tm, zs(-1))

    nxt = (tm + 1) % ntm
    start_1a(0)
    send(lat.at[:, 0], raw.at[2:4, 5], h_send.at[3], h_recv.at[3], tm, zs(-1))
    send(lat.at[:, 3], raw.at[2:4, 0], h_send.at[4], h_recv.at[4], tm, zs(1))
    send(lat.at[:, 0], raw.at[0:2, 1], h_send.at[0], h_recv.at[0], nxt, z)
    send(lat.at[:, 3], raw.at[0:2, 4], h_send.at[1], h_recv.at[1], nxt, z)
    send(lat.at[:, 1:3], raw.at[0:2, 2:4], h_send.at[2], h_recv.at[2], nxt, z)
    start_1a(1)
    acc[...] = jnp.zeros_like(acc)

    col = lax.broadcasted_iota(jnp.int32, (lat.shape[2], chans), 0)

    def shift(i, carry):
        f, r = i // 6, i % 6
        outside = ((r == 0) & (z == 0)) | ((r == 5) & (z == NZ - 1)) | ((f < 2) & (tm == 0))
        keep = jnp.where(outside, 0.0, 1.0).astype(F32)
        v = raw[f, r].astype(F32) * keep
        win[1, f, r] = v.astype(BF16)
        last = lat.shape[2] - 1
        win[0, f, r] = jnp.where(col == 0, 0.0, pltpu.roll(v, 1, 0)).astype(BF16)
        win[2, f, r] = jnp.where(col == last, 0.0, pltpu.roll(v, last, 0)).astype(BF16)
        return carry

    tokens = 2 * 4 * lat.shape[2]
    per_frame = tokens // 2

    def conv(u, lo, hi):
        j, first, count_, *_ = UNITS[u]
        lags = range(first // 9, (first + count_) // 9)

        def step(i, carry):
            dr, dc = i // 3, i % 3
            sums = [None, None]
            for f in range(4):
                pairs = [(g, f - g) for g in range(2) if f - g in lags]
                if not pairs:
                    continue
                patch = win[dc, f, pl.ds(dr, 4)].reshape(per_frame, chans)
                taps = [w[j, :, :, :, 9 * lag + i].reshape(chans, cols) for _, lag in pairs]
                tap = taps[0] if len(taps) == 1 else jnp.concatenate(taps, axis=1)
                term = jnp.dot(patch, tap, preferred_element_type=F32)
                for k, (g, _) in enumerate(pairs):
                    t = term[:, k * cols : (k + 1) * cols]
                    sums[g] = t if sums[g] is None else sums[g] + t
            for g in range(2):
                acc[g] += sums[g]
            return carry

        lax.fori_loop(lo, hi, step, 0)

    lane = lax.broadcasted_iota(jnp.int32, (cols, cols), 0)
    lane2 = lax.broadcasted_iota(jnp.int32, (cols, cols), 1)
    width = chans // GROUPS
    same = (lane // width == lane2 // width).astype(F32)
    count = per_frame * width

    def group_sum(v):
        return jnp.dot(v, same, preferred_element_type=F32, precision=lax.Precision.HIGHEST)

    def finish_chunk(j):
        c = acc[...].astype(BF16)
        acc[...] = jnp.zeros_like(acc)
        kv[j, z] = c
        cf = c.astype(F32)
        mean = group_sum(jnp.sum(cf, axis=1)) * (1.0 / count)
        dev = cf - mean[:, None, :]
        st[z, 0:2, j * cols : (j + 1) * cols] = mean
        st[z, 2:4, j * cols : (j + 1) * cols] = group_sum(jnp.sum(dev * dev, axis=1))
        z_step(j, 0)

    last = CHUNKS - 1
    start_2a(0)
    arrived(raw.at[2:4, 5], h_recv.at[3])
    arrived(raw.at[2:4, 0], h_recv.at[4])
    locals_[0].wait()
    lax.fori_loop(12, 24, shift, 0)
    arrived(raw.at[0:2, 1], h_recv.at[0])
    send(raw.at[0:2, 1], raw.at[0:2, 5], h_send.at[5], h_recv.at[5], tm, zs(-1))
    arrived(raw.at[0:2, 4], h_recv.at[1])
    send(raw.at[0:2, 4], raw.at[0:2, 0], h_send.at[6], h_recv.at[6], tm, zs(1))
    start_1b(1)
    start_1a(2)
    start_2b(0)
    start_1a(3)
    near_lines(0)
    arrived(raw.at[0:2, 5], h_recv.at[5])
    arrived(raw.at[0:2, 0], h_recv.at[6])
    arrived(raw.at[0:2, 2:4], h_recv.at[2])
    lax.fori_loop(0, 12, shift, 0)
    pending.extend((raw.at[0:2, 0], h_send.at[i]) for i in (0, 1, 3, 4, 5, 6))
    pending.append((raw.at[0:2, 0:2], h_send.at[2]))
    start_2a(1)
    start_1b(2)
    finish_gather(0)
    conv(0, 0, 2)
    start_2b(1)
    start_1a(4)
    conv(0, 2, 5)
    start_1b(3)
    start_2a(2)
    conv(0, 5, 9)
    finish_chunk(0)
    near_lines(1)
    finish_gather(1)
    conv(1, 0, 2)
    start_2b(2)
    start_1b(4)
    start_2a(3)
    z_step(0, 1)
    conv(1, 2, 6)
    near_lines(2)
    conv(1, 6, 9)
    z_step(0, 2)
    finish_chunk(1)
    start_2b(3)
    finish_gather(2)
    conv(2, 0, 3)
    z_step(0, 3)
    start_2a(4)
    conv(2, 3, 5)
    z_step(1, 1)
    near_lines(3)
    start_2b(4)
    conv(2, 5, 9)
    z_step(1, 2)
    finish_chunk(2)
    finish_gather(3)
    near_lines(4)
    conv(3, 0, 9)
    z_step(1, 3)
    z_step(2, 1)
    finish_gather(4)
    conv(4, 0, 9)
    finish_chunk(3)

    for d in range(1, NZ):
        send(st.at[z], st.at[z], s_send.at[0], s_recv.at[0], tm, zs(d))
    pending.append((st.at[0 : NZ - 1], s_send.at[0]))
    z_step(2, 2)
    z_step(last, 1)
    arrived(st.at[0 : NZ - 1], s_recv.at[0])
    for c in locals_[1 + CHUNKS :]:
        c.wait()

    means = st[:, 0:2, :]
    mean = jnp.sum(means, axis=0) * (1.0 / NZ)
    apart = means - mean[None]
    spread = jnp.sum(st[:, 2:4, :], axis=0) + count * jnp.sum(apart * apart, axis=0)
    rstd = lax.rsqrt(spread * (1.0 / (count * NZ)) + EPSILON)

    def whole(zb, f):
        return jnp.concatenate([kv[j, zb, f] for j in range(CHUNKS)], axis=1)

    for f in range(2):
        mf, rf = mean[f : f + 1], rstd[f : f + 1]
        n = ((whole(z, f).astype(F32) - mf) * rf).astype(BF16)
        q = jnp.dot(n, wts[0], preferred_element_type=F32).astype(BF16)
        qk = lax.dot_general(q, wts[1], (((1,), (1,)), ((), ())), preferred_element_type=F32)
        qs = (qk * (rf * (LOG2E * chans ** (-0.5)))).astype(BF16)
        qq[f] = qs
        qb[f] = jnp.sum(qs.astype(F32) * mf, axis=1, keepdims=True)

    def attend(blocks, first=False):
        for f in range(2):
            keys = [whole(zb, f) for zb in blocks]
            keys = keys[0] if len(keys) == 1 else jnp.concatenate(keys, axis=0)
            s = lax.dot_general(qq[f], keys, (((1,), (1,)), ((), ())), preferred_element_type=F32)
            s = s - qb[f]
            top = jnp.max(s, axis=1, keepdims=True)
            if not first:
                top = jnp.maximum(top, mx[f])
            p = jnp.exp2(s - top).astype(BF16)
            total = jnp.sum(p.astype(F32), axis=1, keepdims=True)
            part = jnp.dot(p, keys, preferred_element_type=F32)
            if not first:
                scale = jnp.exp2(mx[f] - top)
                total = total + den[f] * scale
                part = part + num[f] * scale
            mx[f] = top
            den[f] = total
            num[f] = part

    attend([z], True)
    z_step(2, 3)
    attend([zs(-1), zs(1)])
    z_step(last, 2)
    attend([zs(-2), zs(2)])
    flush()
    z_step(last, 3)
    attend([zs(-3), zs(3)])
    for j in range(CHUNKS):
        z_step(j, 4)
    attend([zs(4)])

    for f in range(2):
        mf, rf = mean[f : f + 1], rstd[f : f + 1]
        u = ((num[f] / den[f] - mf) * rf).astype(BF16)
        v = jnp.dot(u, wts[2], preferred_element_type=F32).astype(BF16)
        o = whole(z, f).astype(F32) + jnp.dot(v, wts[3], preferred_element_type=F32)
        out[f] = o.astype(BF16).reshape(out.shape[1:])

    flush()


def body(latents, conv_weight, query_weight, key_weight, value_weight, out_weight):
    frames, rows_here, columns, chans = latents.shape
    taps, depth, _ = conv_weight.shape
    tokens = frames * rows_here * columns
    cols = chans // CHUNKS
    dma = pltpu.SemaphoreType.DMA
    return pl.pallas_call(
        kernel,
        out_shape=jax.ShapeDtypeStruct(latents.shape, BF16),
        in_specs=[pl.BlockSpec(memory_space=pl.ANY)] * 6,
        out_specs=pl.BlockSpec(memory_space=pltpu.VMEM),
        scratch_shapes=[
            pltpu.VMEM((4, rows_here + 2, columns, chans), BF16),
            pltpu.VMEM((3, 4, rows_here + 2, columns, chans), BF16),
            pltpu.VMEM((CHUNKS, NX, NY, NC, taps, depth, cols), BF16),
            pltpu.VMEM((CHUNKS, NZ, frames, tokens // frames, cols), BF16),
            pltpu.VMEM((frames, tokens // frames, cols), F32),
            pltpu.VMEM((NZ, 8, chans), F32),
            pltpu.VMEM((4, chans, chans), BF16),
            pltpu.VMEM((frames, tokens // frames, chans), BF16),
            pltpu.VMEM((frames, tokens // frames, 1), F32),
            pltpu.VMEM((frames, tokens // frames, 1), F32),
            pltpu.VMEM((frames, tokens // frames, 1), F32),
            pltpu.VMEM((frames, tokens // frames, chans), F32),
            dma((len(UNITS), 5)), dma((len(UNITS), 17)),
            dma((CHUNKS,)), dma((CHUNKS, 4, 2, 2)),
            dma((7,)), dma((7,)),
            dma((1,)), dma((1,)),
            dma((CHUNKS + 5,)),
        ],
        compiler_params=pltpu.CompilerParams(
            collective_id=0, has_side_effects=True, vmem_limit_bytes=60 * 2**20
        ),
    )(latents, conv_weight, query_weight, key_weight, value_weight, out_weight)


def solution(mesh):
    placed = (P("tm", "rows", None, None), P(None, "tm", None), P(), P(), P(), P())
    return jax.shard_map(
        body, mesh=mesh, in_specs=placed, out_specs=P("tm", "rows", None, None), check_vma=False
    )
```
